32 devices in a mesh: wide: 16 (over z, y, core), narrow: 2 (over x).
Axes of the slice: x: 2, y: 2, z: 4, core: 2. Of those that a mesh axis runs over, the one named last changes fastest.
Arguments:
- voltages: bfloat16 [2, 512, 16, 4096], P(None, 'narrow', 'wide'), may hold values from -6 to 6
- station_flags: int32 [256], replicated, may hold values 0 or 1
- channel_order: int32 [4096], replicated, may hold values from 0 to 4095, each once
- beam_stations: int32 [128, 64], replicated, may hold values from 0 to 255
- beam_weight_re: float32 [128, 64], replicated, may hold values from -0.5 to 0.5
- beam_weight_im: float32 [128, 64], replicated, may hold values from -0.5 to 0.5
Outputs:
- visibilities: float32 [512, 2, 512, 512], P('wide', None, 'narrow')
- beam_power: float32 [4096, 128], P('wide', 'narrow')
The draws below stay inside these ranges and needn't reach their ends.
Inputs may be any that keep to these rules, and one draw needn't show every extreme that they name: `channel_order`: a permutation of the 4096 channel numbers. `beam_stations`: a beam may select a station more than once.
All inputs are finite; a program needn't handle non-finite values.
Results may differ from the reference program's by a relative error of at most 0.0028.
Values may be sent and summed in bfloat16 or wider, within the bound.
A program may use at most 128 MiB of HBM per device.

```python
import math
import jax
import jax.numpy as jnp
from jax import lax

STATIONS = 256
BEAMS = 128
SEL = 64
TAPS = 8
AVG = 8
CH = 4096
INPUTS = 512
FRAMES = 16


def plant(values, own_key, least, largest):
    index_at = [jax.random.randint(jax.random.fold_in(own_key, axis), (), 0, length) for axis, length in enumerate(values.shape)]
    main_axis = values.shape.index(max(values.shape))
    neighbour = index_at[:main_axis] + [(index_at[main_axis] + 1) % values.shape[main_axis]] + index_at[main_axis + 1:]
    return values.at[tuple(index_at)].set(least).at[tuple(neighbour)].set(largest)


def level_of(stream_key, extent, pieces, smallest, high):
    def one(dim, parts):
        draws = jax.random.uniform(jax.random.fold_in(jax.random.fold_in(stream_key, 6), dim), (parts,), jnp.float32, smallest / len(pieces), high / len(pieces))
        return jnp.repeat(jnp.exp(draws), extent[dim] // parts).reshape((-1,) + (1,) * (len(extent) - dim - 1))

    loudness = one(*pieces[0])
    for cut in pieces[1:]:
        loudness = loudness * one(*cut)
    return loudness


def centred(key, extent, width, limit, pieces=(), held_as=jnp.bfloat16):
    result = width * jax.random.normal(key, extent, jnp.float32)
    if pieces:
        result = result * level_of(key, extent, pieces, -0.22, 0.18)
    return jnp.clip(result, -limit, limit).astype(held_as)


def setup_inputs(seed: int = 0) -> dict:
    splits = jax.random.split(jax.random.key(seed), 7)
    return {
        "voltages": centred(splits[0], (2, INPUTS, FRAMES, CH), 1.0, 6.0, ((1, 2), (2, 16))),
        "station_flags": plant((jax.random.randint(splits[1], (STATIONS,), 0, 8) < 7).astype(jnp.int32), jax.random.fold_in(splits[1], 1), 0, 1),
        "channel_order": jax.random.permutation(splits[2], CH).astype(jnp.int32),
        "beam_stations": plant(jax.random.randint(splits[3], (BEAMS, SEL), 0, STATIONS), jax.random.fold_in(splits[3], 1), 0, STATIONS - 1).astype(jnp.int32),
        "beam_weight_re": centred(splits[4], (BEAMS, SEL), (2 * SEL) ** -0.5, 0.5, (), jnp.float32),
        "beam_weight_im": centred(splits[5], (BEAMS, SEL), (2 * SEL) ** -0.5, 0.5, (), jnp.float32),
    }


def prototype(tap_count, length):
    places = jnp.arange(tap_count * length, dtype=jnp.float32)
    offsets = places / length - tap_count / 2.0
    window = 0.5 - 0.5 * jnp.cos(2.0 * jnp.pi * (places + 0.5) / (tap_count * length))
    return (jnp.sinc(offsets) * window).reshape(tap_count, length)

def dense_weights(selection, weight_re, weight_im, station_count):
    beam_count, pick_count = selection.shape
    beam_rows = lax.broadcasted_iota(jnp.int32, (beam_count, pick_count), 0)
    flat_index = (beam_rows * station_count + selection).reshape(-1).astype(jnp.int32)
    summed_re = jax.ops.segment_sum(weight_re.reshape(-1), flat_index, num_segments=beam_count * station_count)
    summed_im = jax.ops.segment_sum(weight_im.reshape(-1), flat_index, num_segments=beam_count * station_count)
    return (summed_re.reshape(beam_count, station_count).astype(jnp.bfloat16), summed_im.reshape(beam_count, station_count).astype(jnp.bfloat16))

def filter_block(volt_block, coefficients, channel_order, input_gain):
    frame_count = volt_block.shape[2]
    tap_count = coefficients.shape[0]
    padded = jnp.pad(volt_block.astype(jnp.float32), ((0, 0), (0, 0), (tap_count - 1, 0), (0, 0)))
    filtered = jnp.zeros(volt_block.shape, jnp.float32)
    for tap_index in range(tap_count):
        begin = tap_count - 1 - tap_index
        filtered = filtered + coefficients[tap_index] * padded[:, :, begin:begin + frame_count, :]
    spectrum = jnp.fft.fft(filtered[0] + 1j * filtered[1], axis=-1) / math.sqrt(volt_block.shape[3])
    chosen = jnp.take(spectrum, channel_order, axis=-1)
    gain_view = input_gain[:, None, None]
    part_re = (jnp.real(chosen) * gain_view).astype(jnp.bfloat16)
    part_im = (jnp.imag(chosen) * gain_view).astype(jnp.bfloat16)
    return jnp.stack([part_re, part_im], axis=0)

def reference(voltages, station_flags, channel_order, beam_stations, beam_weight_re, beam_weight_im):
    input_count = voltages.shape[1]
    frame_count = voltages.shape[2]
    length = voltages.shape[3]
    coefficients = prototype(TAPS, length)
    input_gain = jnp.repeat(station_flags, 2).astype(jnp.float32)
    block_count = math.gcd(input_count, 16)
    block_size = input_count // block_count
    volt_blocks = voltages.reshape(2, block_count, block_size, frame_count, length).transpose(1, 0, 2, 3, 4)
    gain_blocks = input_gain.reshape(block_count, block_size)

    def channelize(entry_pair):
        return filter_block(entry_pair[0], coefficients, channel_order, entry_pair[1])
    spectra = lax.map(channelize, (volt_blocks, gain_blocks))
    spectra = spectra.transpose(1, 0, 2, 3, 4).reshape(2, input_count, frame_count, length)
    group_count = length // AVG
    grouped = spectra.reshape(2, input_count, frame_count, group_count, AVG).transpose(3, 0, 1, 2, 4)
    matrix_re, matrix_im = dense_weights(beam_stations, beam_weight_re, beam_weight_im, input_count // 2)
    vis_scale = 1.0 / math.sqrt(AVG * frame_count)

    def correlate(group_entry):
        rows_re = group_entry[0].reshape(input_count, frame_count * AVG)
        rows_im = group_entry[1].reshape(input_count, frame_count * AVG)
        vis_re = jnp.dot(rows_re, rows_re.T, preferred_element_type=jnp.float32) + jnp.dot(rows_im, rows_im.T, preferred_element_type=jnp.float32)
        vis_im = jnp.dot(rows_im, rows_re.T, preferred_element_type=jnp.float32) - jnp.dot(rows_re, rows_im.T, preferred_element_type=jnp.float32)
        vis_pair = jnp.stack([vis_re, vis_im], axis=0) * vis_scale
        station_re = group_entry[0].reshape(input_count // 2, 2 * frame_count * AVG)
        station_im = group_entry[1].reshape(input_count // 2, 2 * frame_count * AVG)
        beam_re = jnp.dot(matrix_re, station_re, preferred_element_type=jnp.float32) - jnp.dot(matrix_im, station_im, preferred_element_type=jnp.float32)
        beam_im = jnp.dot(matrix_re, station_im, preferred_element_type=jnp.float32) + jnp.dot(matrix_im, station_re, preferred_element_type=jnp.float32)
        energy = (beam_re * beam_re + beam_im * beam_im).reshape(-1, 2, frame_count, AVG)
        energy = lax.optimization_barrier(jnp.sum(energy, axis=(1, 2))) / frame_count
        return (vis_pair, energy)
    visibilities, energies = lax.map(correlate, grouped)
    beam_power = energies.transpose(0, 2, 1).reshape(length, -1)
    return (visibilities, beam_power)
```

```python
import functools
import math

import jax
import jax.numpy as jnp
import numpy as np
from jax import lax
from jax.experimental import pallas as pl
from jax.experimental.pallas import tpu as pltpu
from jax.sharding import PartitionSpec as P

TAPS = 8
AVG = 8
LANES = 128


def prototype(tap_count, length):
    places = np.arange(tap_count * length)
    offsets = places / length - tap_count / 2.0
    window = 0.5 - 0.5 * np.cos(2.0 * np.pi * (places + 0.5) / (tap_count * length))
    return (np.sinc(offsets) * window).astype(np.float32).reshape(tap_count, length)


def dense_weights(selection, weight_re, weight_im, station_count):
    beam_count, pick_count = selection.shape
    beam_rows = lax.broadcasted_iota(jnp.int32, (beam_count, pick_count), 0)
    flat_index = (beam_rows * station_count + selection).reshape(-1)
    summed_re = jax.ops.segment_sum(
        weight_re.reshape(-1), flat_index, num_segments=beam_count * station_count
    )
    summed_im = jax.ops.segment_sum(
        weight_im.reshape(-1), flat_index, num_segments=beam_count * station_count
    )
    return (
        summed_re.reshape(beam_count, station_count).astype(jnp.bfloat16),
        summed_im.reshape(beam_count, station_count).astype(jnp.bfloat16),
    )


def transform(filtered):
    input_count, frame_count, length = (filtered.shape[1], filtered.shape[2], filtered.shape[3])
    section_size = math.isqrt(length)
    counter = jnp.arange(section_size, dtype=jnp.int32)
    products = counter[:, None] * counter[None, :]
    section_angle = 2.0 * math.pi / section_size * (products % section_size).astype(jnp.float32)
    twist_angle = 2.0 * math.pi / length * products.astype(jnp.float32)
    cosine = jnp.cos(section_angle)
    sine_table = jnp.sin(section_angle)
    twist_cos = jnp.cos(twist_angle)
    twist_sin = jnp.sin(twist_angle)
    mixing = jnp.concatenate(
        [
            jnp.concatenate([cosine, -sine_table], axis=1),
            jnp.concatenate([sine_table, cosine], axis=1),
        ],
        axis=0,
    )
    twist_scale = jnp.concatenate([twist_cos, twist_cos], axis=1)
    twist_cross = jnp.concatenate([twist_sin, -twist_sin], axis=1)
    sample_grid = filtered.reshape(2, input_count, frame_count, section_size, section_size)
    stacked = jnp.moveaxis(sample_grid, 0, 3).reshape(
        input_count, frame_count, section_size, 2 * section_size
    )
    first_pass = jnp.einsum("cn,ifnk->ifck", cosine, stacked, precision=lax.Precision.HIGHEST)
    second_pass = jnp.einsum("cn,ifnk->ifck", sine_table, stacked, precision=lax.Precision.HIGHEST)
    sectioned = first_pass + jnp.concatenate(
        [second_pass[..., section_size:], -second_pass[..., :section_size]], axis=-1
    )
    swapped = jnp.concatenate(
        [sectioned[..., section_size:], sectioned[..., :section_size]], axis=-1
    )
    twisted = sectioned * twist_scale + swapped * twist_cross
    result = jnp.einsum("ifck,kj->ifcj", twisted, mixing, precision=lax.Precision.HIGHEST)
    return result * (1.0 / math.sqrt(length))


def row_stack(grouped):
    part_re, part_im = (grouped[0], grouped[1])
    return jnp.stack(
        [jnp.stack([part_re, part_im], axis=2), jnp.stack([part_im, -part_re], axis=2)], axis=0
    )


def apply_taps_long(extended, coefficients, frame_count):
    result = jnp.zeros(extended.shape[:2] + (frame_count, extended.shape[3]), jnp.float32)
    for tap_index in range(TAPS):
        begin = TAPS - 1 - tap_index
        result = result + coefficients[tap_index] * extended[
            :, :, begin : begin + frame_count
        ].astype(jnp.float32)
    return result


def shards(voltages, station_flags, channel_order, beam_stations, beam_weight_re, beam_weight_im):
    local_inputs = voltages.shape[1]
    frame_count = voltages.shape[2]
    length = voltages.shape[3]
    section_size = math.isqrt(length)
    coefficients = prototype(TAPS, length)
    across = lax.all_to_all(voltages, "wide", split_axis=3, concat_axis=2, tiled=True)
    column_count = across.shape[3]
    total_frames = across.shape[2]
    own_coeffs = lax.dynamic_slice_in_dim(
        coefficients, lax.axis_index("wide") * column_count, column_count, axis=1
    )
    padded = jnp.pad(across, ((0, 0), (0, 0), (TAPS - 1, 0), (0, 0)))
    local_filtered = apply_taps_long(padded, own_coeffs, total_frames)
    filtered = lax.all_to_all(local_filtered, "wide", split_axis=2, concat_axis=3, tiled=True)
    spectrum = transform(filtered)
    layout = spectrum.reshape(local_inputs, frame_count, section_size, 2, section_size)
    layout = jnp.transpose(layout, (3, 0, 2, 4, 1)).reshape(2, local_inputs, length, frame_count)
    local_stations = local_inputs // 2
    own_flags = lax.dynamic_slice_in_dim(
        station_flags, lax.axis_index("narrow") * local_stations, local_stations
    )
    input_gain = jnp.repeat(own_flags, 2).astype(jnp.float32)
    rounded = (layout * input_gain[None, :, None, None]).astype(jnp.bfloat16)
    position = channel_order % section_size * section_size + channel_order // section_size
    chosen = (position[:, None] == jnp.arange(length)[None, :]).astype(jnp.bfloat16)
    spectra = jnp.einsum('pk,rikf->ripf', chosen, rounded)
    turned = lax.all_to_all(spectra, "wide", split_axis=2, concat_axis=3, tiled=True)
    local_channels = turned.shape[2]
    all_frames = turned.shape[3]
    group_count = local_channels // AVG
    contraction = AVG * all_frames
    grouped = turned.reshape(2, local_inputs, group_count, contraction)
    vis_scale = 1.0 / math.sqrt(contraction)
    matrix_re, matrix_im = dense_weights(
        beam_stations, beam_weight_re, beam_weight_im, station_flags.shape[0]
    )
    beam_block = jnp.stack(
        [jnp.stack([matrix_re, -matrix_im], axis=1), jnp.stack([matrix_im, matrix_re], axis=1)],
        axis=0,
    )
    narrow_count = lax.axis_size("narrow")
    beam_local = beam_block.shape[1] // narrow_count
    own_beams = lax.dynamic_slice_in_dim(
        beam_block, lax.axis_index("narrow") * beam_local, beam_local, axis=1
    )
    left_rows = row_stack(grouped)
    shard_piece = lax.all_gather(grouped, "narrow", axis=1, tiled=True)
    columns = jnp.einsum(
        "rivqk,qjvk->vrij", left_rows, shard_piece, preferred_element_type=jnp.float32
    )
    piece_stations = shard_piece.shape[1] // 2
    voices = shard_piece.reshape(2, piece_stations, 2, group_count, contraction)
    beam_running = jnp.einsum(
        "obps,pslvk->oblvk", own_beams, voices, preferred_element_type=jnp.float32
    )
    visibilities = columns * vis_scale
    beam_energy = jnp.sum(beam_running * beam_running, axis=(0, 2)).reshape(
        beam_local, group_count, AVG, all_frames
    )
    beam_energy = jnp.sum(beam_energy, axis=3).reshape(beam_local, local_channels) / all_frames
    beam_power = beam_energy.T
    return (visibilities, beam_power)


def phase_table(rows, columns, period):
    products = np.arange(rows)[:, None] * np.arange(columns)[None, :]
    angle = 2.0 * np.pi / period * (products % period)
    return np.cos(angle).astype(np.float32), np.sin(angle).astype(np.float32)


def short_fft(parts):
    count = len(parts)
    if count == 1:
        return parts
    even = short_fft(parts[0::2])
    odd = short_fft(parts[1::2])
    low, high = [], []
    for place in range(count // 2):
        (even_re, even_im), (odd_re, odd_im) = even[place], odd[place]
        if place == 0:
            turn_re, turn_im = odd_re, odd_im
        elif 4 * place == count:
            turn_re, turn_im = odd_im, -odd_re
        else:
            cosine = math.cos(2.0 * math.pi * place / count)
            sine = math.sin(2.0 * math.pi * place / count)
            turn_re = cosine * odd_re + sine * odd_im
            turn_im = cosine * odd_im - sine * odd_re
        low.append((even_re + turn_re, even_im + turn_im))
        high.append((even_re - turn_re, even_im - turn_im))
    return low + high


def swap_octet(blocks):
    lane = lax.broadcasted_iota(jnp.int32, blocks[0].shape, 1)
    width = blocks[0].shape[1]
    for step in (1, 2, 4):
        keep = lane & step == 0
        swapped = list(blocks)
        for low in range(8):
            if low & step == 0:
                high = low + step
                swapped[low] = jnp.where(keep, blocks[low], pltpu.roll(blocks[high], step, 1))
                swapped[high] = jnp.where(keep, pltpu.roll(blocks[low], width - step, 1), blocks[high])
        blocks = swapped
    return blocks


def flip(place, mask, count):
    result, step = 0, 1
    while step < count:
        bit = place // step % 2
        result = result + step * (1 - bit if mask & step else bit)
        step *= 2
    return result


def channelize(half, hooks, refs, scratch):
    rows_ref, coef_ref, gain_ref, twist_cos_ref, twist_sin_ref, w_high_ref, w_low_ref = refs
    received, filt, stage, spec, picked, turned, spectra = scratch
    frames, _, inputs, length = received.shape[1:]
    sections = length // LANES
    hooks = list(hooks)

    def staged(total, pieces, unroll):
        size = total // pieces

        def run(body):
            for piece in range(pieces):
                pl.loop(piece * size, (piece + 1) * size, unroll=unroll)(body)
                if hooks:
                    hooks.pop(0)()

        return run

    @staged(sections, 2, 1)
    def _(section):
        lanes = pl.ds(pl.multiple_of(section * LANES, LANES), LANES)
        taps = [coef_ref[k : k + 1, lanes] for k in range(TAPS)]
        for part in range(2):
            window = []
            for frame in range(frames):
                window = [received[half, frame, part, :, lanes].astype(jnp.float32)] + window[: TAPS - 1]
                total = taps[0] * window[0]
                for k in range(1, len(window)):
                    total = total + taps[k] * window[k]
                filt[section, part, frame] = total

    @staged(frames, 2, 1)
    def _(frame):
        values = [(filt[s, 0, frame], filt[s, 1, frame]) for s in range(sections)]
        row = pl.multiple_of(frame * 8, 8)
        for c, (re, im) in enumerate(short_fft(values)):
            cosine, sine = twist_cos_ref[c : c + 1, :], twist_sin_ref[c : c + 1, :]
            stage[c, pl.ds(row, 8), :LANES] = re * cosine + im * sine
            stage[c, pl.ds(row, 8), LANES:] = im * cosine - re * sine

    over_lanes = (((1,), (1,)), ((), ()))

    @staged(sections, 2, 4)
    def _(c):
        value = stage[c]
        high = value.astype(jnp.bfloat16)
        low = (value - high.astype(jnp.float32)).astype(jnp.bfloat16)
        w_high, w_low = w_high_ref[...], w_low_ref[...]
        result = lax.dot_general(w_high, high, over_lanes, preferred_element_type=jnp.float32)
        result += lax.dot_general(w_high, low, over_lanes, preferred_element_type=jnp.float32)
        result += lax.dot_general(w_low, high, over_lanes, preferred_element_type=jnp.float32)
        result = result * gain_ref[half : half + 1, :]
        place = pl.ds(pl.multiple_of(c * LANES, LANES), LANES)
        spec[place, : frames * inputs] = result[:LANES]
        spec[place, frames * inputs :] = result[LANES:]

    @staged(length // 64, 2, 1)
    def _(step):
        base = pl.multiple_of(step * 64, 64)
        for begin in range(0, 64, 16):
            rows = [spec[pl.ds(rows_ref[base + begin + j], 1), :] for j in range(16)]
            for j, row in enumerate(rows):
                group, place = divmod(begin + j, 8)
                picked[pl.ds(base + place * 8 + group, 1), :] = row

    depth = 2 * inputs

    @staged(length // 64, 2, 2)
    def _(step):
        base = pl.multiple_of(step * 64, 64)
        target = pl.multiple_of(step * (8 * depth), 8 * depth)
        for part in range(2):
            lanes = slice(part * LANES, (part + 1) * LANES)
            blocks = [picked[pl.ds(base + place * 8, 8), lanes] for place in range(8)]
            for i, block in enumerate(swap_octet(blocks)):
                turned[pl.ds(target + part * inputs + i, 8, stride=depth), :] = block

    @staged(length // 64, 1, 4)
    def _(step):
        target = pl.multiple_of(step * (8 * depth), 8 * depth)
        rounded = turned[pl.ds(target, 8 * depth), :].astype(jnp.bfloat16)
        spectra[half, pl.ds(step * 8, 8)] = rounded.reshape(8, depth, LANES)

    for hook in hooks:
        hook()


def turn_kernel(
    count, near_count, in_flight,
    rows_ref, volt_ref, coef_ref, gain_ref, twist_cos_ref, twist_sin_ref, w_high_ref, w_low_ref,
    out_ref,
    received, filt, stage, spec, picked, turned, spectra,
    in_local, in_send, in_recv, out_local, out_send, out_recv, cross_send, cross_recv,
):
    me, side = lax.axis_index("wide"), lax.axis_index("narrow")
    mesh_ids = pl.DeviceIdType.MESH
    groups = spectra.shape[1] // count
    barrier = pltpu.get_barrier_semaphore()
    for mask in range(1, count):
        pl.semaphore_signal(barrier, inc=1, device_id={"wide": flip(me, mask, count)}, device_id_type=mesh_ids)
    for mask in range(near_count):
        target = {"wide": flip(me, mask, count), "narrow": 1 - side}
        pl.semaphore_signal(barrier, inc=1, device_id=target, device_id_type=mesh_ids)
    pl.semaphore_wait(barrier, count - 1 + near_count)

    def entering(half, mask):
        peer = flip(me, mask, count)
        return pltpu.make_async_remote_copy(
            src_ref=volt_ref.at[:, peer, half],
            dst_ref=received.at[half, me],
            send_sem=in_send.at[half, mask],
            recv_sem=in_recv.at[half, mask],
            device_id={"wide": peer},
            device_id_type=mesh_ids,
        )

    def entered(half, mask):
        peer = flip(me, mask, count)
        return pltpu.make_async_remote_copy(
            src_ref=volt_ref.at[:, peer, half],
            dst_ref=received.at[half, peer],
            send_sem=in_send.at[half, mask],
            recv_sem=in_recv.at[half, mask],
            device_id={"wide": peer},
            device_id_type=mesh_ids,
        )

    def kept_in(half):
        return pltpu.make_async_copy(volt_ref.at[:, me, half], received.at[half, me], in_local.at[half])

    def kept_out(half):
        return pltpu.make_async_copy(
            spectra.at[half, pl.ds(me * groups, groups)], out_ref.at[side, me, half], out_local.at[half]
        )

    def outgoing(half, mask):
        peer = flip(me, mask, count)
        return pltpu.make_async_remote_copy(
            src_ref=spectra.at[half, pl.ds(peer * groups, groups)],
            dst_ref=out_ref.at[side, me, half],
            send_sem=out_send.at[half, mask],
            recv_sem=out_recv.at[half, mask],
            device_id={"wide": peer},
            device_id_type=mesh_ids,
        )

    def arriving(half, mask):
        peer = flip(me, mask, count)
        return pltpu.make_async_remote_copy(
            src_ref=spectra.at[half, pl.ds(peer * groups, groups)],
            dst_ref=out_ref.at[side, peer, half],
            send_sem=out_send.at[half, mask],
            recv_sem=out_recv.at[half, mask],
            device_id={"wide": peer},
            device_id_type=mesh_ids,
        )

    def across(half, mask):
        peer = flip(me, mask, count)
        if mask < near_count:
            source = spectra.at[half, pl.ds(peer * groups, groups)]
            target = out_ref.at[side, me, half]
            device = {"wide": peer, "narrow": 1 - side}
        else:
            source = target = out_ref.at[side, peer, half]
            device = {"narrow": 1 - side}
        return pltpu.make_async_remote_copy(
            src_ref=source,
            dst_ref=target,
            send_sem=cross_send.at[half, mask],
            recv_sem=cross_recv.at[half, mask],
            device_id=device,
            device_id_type=mesh_ids,
        )

    def crossed(half, mask):
        peer = flip(me, mask, count)
        landed = out_ref.at[1 - side, peer, half]
        return pltpu.make_async_remote_copy(
            src_ref=landed,
            dst_ref=landed,
            send_sem=cross_send.at[half, mask],
            recv_sem=cross_recv.at[half, mask],
            device_id={"narrow": 1 - side},
            device_id_type=mesh_ids,
        )

    near = list(range(1, near_count))
    far = list(range(near_count, count))
    refs = (rows_ref, coef_ref, gain_ref, twist_cos_ref, twist_sin_ref, w_high_ref, w_low_ref)
    scratch = (received, filt, stage, spec, picked, turned, spectra)

    def enter(half):
        for mask in far + near:
            entering(half, mask).start()
        kept_in(half).start()

    def await_entry(half):
        kept_in(half).wait()
        for mask in far + near:
            entering(half, mask).wait_send()
        for mask in far + near:
            entered(half, mask).wait_recv()

    def leave(half):
        for mask in far[:in_flight]:
            outgoing(half, mask).start()
        for mask in near:
            outgoing(half, mask).start()
        for mask in range(near_count):
            across(half, mask).start()
        kept_out(half).start()

    def pass_on(half, place):
        def step():
            outgoing(half, far[place]).wait_send()
            if place + in_flight < len(far):
                outgoing(half, far[place + in_flight]).start()
            arriving(half, far[place]).wait_recv()
            across(half, far[place]).start()

        return step

    enter(0)
    await_entry(0)
    enter(1)
    channelize(0, [], refs, scratch)
    leave(0)
    await_entry(1)
    channelize(1, [pass_on(0, place) for place in range(len(far))], refs, scratch)
    leave(1)
    for place in range(len(far)):
        pass_on(1, place)()
    for half in range(2):
        kept_out(half).wait()
        for mask in near:
            outgoing(half, mask).wait_send()
            arriving(half, mask).wait_recv()
        for mask in range(count):
            across(half, mask).wait_send()
            crossed(half, mask).wait_recv()


def turn(voltages, rows, coefficients, gain, near_count, in_flight):
    _, count, halves, inputs, length = voltages.shape
    frames = count
    sections = length // LANES
    twist_cos, twist_sin = phase_table(sections, LANES, length)
    cosine, sine = phase_table(LANES, LANES, LANES)
    weights = np.concatenate(
        [np.concatenate([cosine, sine], axis=1), np.concatenate([-sine, cosine], axis=1)], axis=0
    ) / np.float32(math.sqrt(length))
    w_high = weights.astype(jnp.bfloat16)
    w_low = (weights - w_high.astype(np.float32)).astype(jnp.bfloat16)
    whole = pl.BlockSpec(memory_space=pltpu.VMEM)
    anywhere = pl.BlockSpec(memory_space=pl.ANY)
    depth = 2 * inputs
    pair = pltpu.SemaphoreType.DMA((halves,))
    table = pltpu.SemaphoreType.DMA((halves, count))
    return pl.pallas_call(
        functools.partial(turn_kernel, count, near_count, in_flight),
        out_shape=jax.ShapeDtypeStruct((2, count, halves, length // AVG // count, depth, LANES), jnp.bfloat16),
        in_specs=[pl.BlockSpec(memory_space=pltpu.SMEM), anywhere] + [whole] * 6,
        out_specs=anywhere,
        scratch_shapes=[
            pltpu.VMEM((halves, frames, 2, inputs, length), jnp.bfloat16),
            pltpu.VMEM((sections, 2, frames, inputs, LANES), jnp.float32),
            pltpu.VMEM((sections, frames * inputs, 2 * LANES), jnp.float32),
            pltpu.VMEM((length, 2 * frames * inputs), jnp.float32),
            pltpu.VMEM((length, 2 * frames * inputs), jnp.float32),
            pltpu.VMEM((length // 8 * depth, LANES), jnp.float32),
            pltpu.VMEM((halves, length // 8, depth, LANES), jnp.bfloat16),
            pair, table, table, pair, table, table, table, table,
        ],
        compiler_params=pltpu.CompilerParams(
            collective_id=0, has_side_effects=True, vmem_limit_bytes=60 * 2**20
        ),
        name="turn",
    )(rows, voltages, coefficients, gain, twist_cos, twist_sin, jnp.asarray(w_high), jnp.asarray(w_low))


def parts_of(block):
    rows = block.reshape(-1, 16, LANES).astype(jnp.float32)
    return [
        rows[:, begin : begin + 8].reshape(-1, LANES).astype(jnp.bfloat16) for begin in (0, 8)
    ]


def correlate_kernel(scale, frame_count, side_ref, all_ref, beam_ref, vis_ref, power_ref):
    over_lanes = (((1,), (1,)), ((), ()))
    count = power_ref.shape[1]
    stacked = []
    for group in range(vis_ref.shape[0]):
        own_re, own_im = parts_of(all_ref[side_ref[0], :, :, group])
        re, im = parts_of(all_ref[:, :, :, group])
        both = jnp.concatenate([re, im], axis=1)
        left_re = jnp.concatenate([own_re, own_im], axis=1)
        left_im = jnp.concatenate([own_im, -own_re], axis=1)
        vis_ref[group, 0] = scale * lax.dot_general(
            left_re, both, over_lanes, preferred_element_type=jnp.float32
        )
        vis_ref[group, 1] = scale * lax.dot_general(
            left_im, both, over_lanes, preferred_element_type=jnp.float32
        )
        stacked.append(jnp.concatenate([re, im], axis=0))
    beam = jnp.dot(
        beam_ref[...], jnp.concatenate(stacked, axis=1), preferred_element_type=jnp.float32
    )
    energy = beam * beam
    total = energy[:count]
    for piece in range(1, energy.shape[0] // count):
        total = total + energy[piece * count : (piece + 1) * count]
    place = lax.broadcasted_iota(jnp.int32, (AVG, LANES), 0)
    lane = lax.broadcasted_iota(jnp.int32, (AVG, LANES), 1)
    pick = (lane % AVG == place).astype(jnp.float32)
    for group in range(vis_ref.shape[0]):
        power_ref[group * AVG : (group + 1) * AVG, :] = (
            lax.dot_general(
                pick,
                total[:, group * LANES : (group + 1) * LANES],
                over_lanes,
                precision=lax.Precision.HIGHEST,
                preferred_element_type=jnp.float32,
            )
            / frame_count
        )


def correlate(gathered, side, beam_rows, beam_local, frame_count):
    sides, sources, halves, groups, depth, _ = gathered.shape
    rows = sources * halves * 8
    batch = math.gcd(groups, 4)
    return pl.pallas_call(
        functools.partial(correlate_kernel, 1.0 / math.sqrt(AVG * frame_count), frame_count),
        grid_spec=pltpu.PrefetchScalarGridSpec(
            num_scalar_prefetch=1,
            grid=(groups // batch,),
            in_specs=[
                pl.BlockSpec((sides, sources, halves, batch, depth, LANES), lambda v, at: (0, 0, 0, v, 0, 0)),
                pl.BlockSpec(beam_rows.shape, lambda v, at: (0, 0)),
            ],
            out_specs=(
                pl.BlockSpec((batch, 2, rows, sides * rows), lambda v, at: (v, 0, 0, 0)),
                pl.BlockSpec((batch * AVG, beam_local), lambda v, at: (v, 0)),
            ),
        ),
        out_shape=(
            jax.ShapeDtypeStruct((groups, 2, rows, sides * rows), jnp.float32),
            jax.ShapeDtypeStruct((groups * AVG, beam_local), jnp.float32),
        ),
        compiler_params=pltpu.CompilerParams(vmem_limit_bytes=60 * 2**20),
        name="correlate",
    )(side.reshape(1), gathered, beam_rows)


def beam_block_rows(selection, weight_re, weight_im, station_count):
    hit = selection[:, :, None] == jnp.arange(station_count, dtype=jnp.int32)[None, None, :]
    matrix_re = jnp.sum(jnp.where(hit, weight_re[:, :, None], 0.0), axis=1).astype(jnp.bfloat16)
    matrix_im = jnp.sum(jnp.where(hit, weight_im[:, :, None], 0.0), axis=1).astype(jnp.bfloat16)

    def spread(matrix):
        zero = jnp.zeros_like(matrix)
        first = jnp.stack([matrix, zero], axis=2).reshape(matrix.shape[0], -1)
        second = jnp.stack([zero, matrix], axis=2).reshape(matrix.shape[0], -1)
        return jnp.concatenate([first, second], axis=0)

    wide_re, wide_im = spread(matrix_re), spread(matrix_im)
    return jnp.concatenate(
        [
            jnp.concatenate([wide_re, -wide_im], axis=1),
            jnp.concatenate([wide_im, wide_re], axis=1),
        ],
        axis=0,
    )


def fast_shards(voltages, station_flags, channel_order, beam_stations, beam_weight_re, beam_weight_im):
    local_inputs, frames, length = voltages.shape[1:]
    devices = lax.axis_size("wide")
    share = local_inputs // devices
    sections = length // LANES
    narrow = lax.axis_index("narrow")
    first = narrow * local_inputs + lax.axis_index("wide") * share
    gain = lax.dynamic_slice_in_dim(jnp.repeat(station_flags, 2), first, share).astype(jnp.float32)
    gain = jnp.tile(gain.reshape(2, share // 2), (1, devices * frames))
    rows = channel_order % sections * LANES + channel_order // sections
    blocks = voltages.reshape(2, devices, 2, share // 2, length)
    gathered = turn(blocks, rows, prototype(TAPS, length), gain, devices // 2, 4)
    beam_local = beam_stations.shape[0] // lax.axis_size("narrow")
    picks = [
        lax.dynamic_slice_in_dim(table, narrow * beam_local, beam_local)
        for table in (beam_stations, beam_weight_re, beam_weight_im)
    ]
    beam_rows = beam_block_rows(*picks, station_flags.shape[0])
    return correlate(gathered, narrow, beam_rows, beam_local, devices * frames)


def solution(mesh):
    def body(*args):
        local_inputs, frames, length = args[0].shape[1:]
        devices = mesh.shape["wide"]
        share = local_inputs // devices
        sections = length // LANES
        fits = (
            frames == 1
            and local_inputs % devices == 0
            and share == 16
            and mesh.shape["narrow"] == 2
            and devices * AVG == LANES
            and length % (LANES * devices) == 0
            and sections & (sections - 1) == 0
        )
        return (fast_shards if fits else shards)(*args)

    return jax.shard_map(
        body,
        mesh=mesh,
        in_specs=(P(None, "narrow", "wide", None), P(), P(), P(), P(), P()),
        out_specs=(P("wide", None, "narrow", None), P("wide", "narrow")),
        check_vma=False,
    )
```

```python
import functools
import math

import jax
import jax.numpy as jnp
import numpy as np
from jax import lax
from jax.experimental import pallas as pl
from jax.experimental.pallas import tpu as pltpu
from jax.sharding import PartitionSpec as P

TAPS = 8
AVG = 8
LANES = 128


def prototype(tap_count, length):
    places = np.arange(tap_count * length)
    offsets = places / length - tap_count / 2.0
    window = 0.5 - 0.5 * np.cos(2.0 * np.pi * (places + 0.5) / (tap_count * length))
    return (np.sinc(offsets) * window).astype(np.float32).reshape(tap_count, length)


def dense_weights(selection, weight_re, weight_im, station_count):
    beam_count, pick_count = selection.shape
    beam_rows = lax.broadcasted_iota(jnp.int32, (beam_count, pick_count), 0)
    flat_index = (beam_rows * station_count + selection).reshape(-1)
    summed_re = jax.ops.segment_sum(
        weight_re.reshape(-1), flat_index, num_segments=beam_count * station_count
    )
    summed_im = jax.ops.segment_sum(
        weight_im.reshape(-1), flat_index, num_segments=beam_count * station_count
    )
    return (
        summed_re.reshape(beam_count, station_count).astype(jnp.bfloat16),
        summed_im.reshape(beam_count, station_count).astype(jnp.bfloat16),
    )


def transform(filtered):
    input_count, frame_count, length = (filtered.shape[1], filtered.shape[2], filtered.shape[3])
    section_size = math.isqrt(length)
    counter = jnp.arange(section_size, dtype=jnp.int32)
    products = counter[:, None] * counter[None, :]
    section_angle = 2.0 * math.pi / section_size * (products % section_size).astype(jnp.float32)
    twist_angle = 2.0 * math.pi / length * products.astype(jnp.float32)
    cosine = jnp.cos(section_angle)
    sine_table = jnp.sin(section_angle)
    twist_cos = jnp.cos(twist_angle)
    twist_sin = jnp.sin(twist_angle)
    mixing = jnp.concatenate(
        [
            jnp.concatenate([cosine, -sine_table], axis=1),
            jnp.concatenate([sine_table, cosine], axis=1),
        ],
        axis=0,
    )
    twist_scale = jnp.concatenate([twist_cos, twist_cos], axis=1)
    twist_cross = jnp.concatenate([twist_sin, -twist_sin], axis=1)
    sample_grid = filtered.reshape(2, input_count, frame_count, section_size, section_size)
    stacked = jnp.moveaxis(sample_grid, 0, 3).reshape(
        input_count, frame_count, section_size, 2 * section_size
    )
    first_pass = jnp.einsum("cn,ifnk->ifck", cosine, stacked, precision=lax.Precision.HIGHEST)
    second_pass = jnp.einsum("cn,ifnk->ifck", sine_table, stacked, precision=lax.Precision.HIGHEST)
    sectioned = first_pass + jnp.concatenate(
        [second_pass[..., section_size:], -second_pass[..., :section_size]], axis=-1
    )
    swapped = jnp.concatenate(
        [sectioned[..., section_size:], sectioned[..., :section_size]], axis=-1
    )
    twisted = sectioned * twist_scale + swapped * twist_cross
    result = jnp.einsum("ifck,kj->ifcj", twisted, mixing, precision=lax.Precision.HIGHEST)
    return result * (1.0 / math.sqrt(length))


def row_stack(grouped):
    part_re, part_im = (grouped[0], grouped[1])
    return jnp.stack(
        [jnp.stack([part_re, part_im], axis=2), jnp.stack([part_im, -part_re], axis=2)], axis=0
    )


def apply_taps_long(extended, coefficients, frame_count):
    result = jnp.zeros(extended.shape[:2] + (frame_count, extended.shape[3]), jnp.float32)
    for tap_index in range(TAPS):
        begin = TAPS - 1 - tap_index
        result = result + coefficients[tap_index] * extended[
            :, :, begin : begin + frame_count
        ].astype(jnp.float32)
    return result


def shards(voltages, station_flags, channel_order, beam_stations, beam_weight_re, beam_weight_im):
    local_inputs = voltages.shape[1]
    frame_count = voltages.shape[2]
    length = voltages.shape[3]
    section_size = math.isqrt(length)
    coefficients = prototype(TAPS, length)
    across = lax.all_to_all(voltages, "wide", split_axis=3, concat_axis=2, tiled=True)
    column_count = across.shape[3]
    total_frames = across.shape[2]
    own_coeffs = lax.dynamic_slice_in_dim(
        coefficients, lax.axis_index("wide") * column_count, column_count, axis=1
    )
    padded = jnp.pad(across, ((0, 0), (0, 0), (TAPS - 1, 0), (0, 0)))
    local_filtered = apply_taps_long(padded, own_coeffs, total_frames)
    filtered = lax.all_to_all(local_filtered, "wide", split_axis=2, concat_axis=3, tiled=True)
    spectrum = transform(filtered)
    layout = spectrum.reshape(local_inputs, frame_count, section_size, 2, section_size)
    layout = jnp.transpose(layout, (3, 0, 2, 4, 1)).reshape(2, local_inputs, length, frame_count)
    local_stations = local_inputs // 2
    own_flags = lax.dynamic_slice_in_dim(
        station_flags, lax.axis_index("narrow") * local_stations, local_stations
    )
    input_gain = jnp.repeat(own_flags, 2).astype(jnp.float32)
    rounded = (layout * input_gain[None, :, None, None]).astype(jnp.bfloat16)
    position = channel_order % section_size * section_size + channel_order // section_size
    chosen = (position[:, None] == jnp.arange(length)[None, :]).astype(jnp.bfloat16)
    spectra = jnp.einsum('pk,rikf->ripf', chosen, rounded)
    turned = lax.all_to_all(spectra, "wide", split_axis=2, concat_axis=3, tiled=True)
    local_channels = turned.shape[2]
    all_frames = turned.shape[3]
    group_count = local_channels // AVG
    contraction = AVG * all_frames
    grouped = turned.reshape(2, local_inputs, group_count, contraction)
    vis_scale = 1.0 / math.sqrt(contraction)
    matrix_re, matrix_im = dense_weights(
        beam_stations, beam_weight_re, beam_weight_im, station_flags.shape[0]
    )
    beam_block = jnp.stack(
        [jnp.stack([matrix_re, -matrix_im], axis=1), jnp.stack([matrix_im, matrix_re], axis=1)],
        axis=0,
    )
    narrow_count = lax.axis_size("narrow")
    beam_local = beam_block.shape[1] // narrow_count
    own_beams = lax.dynamic_slice_in_dim(
        beam_block, lax.axis_index("narrow") * beam_local, beam_local, axis=1
    )
    left_rows = row_stack(grouped)
    shard_piece = lax.all_gather(grouped, "narrow", axis=1, tiled=True)
    columns = jnp.einsum(
        "rivqk,qjvk->vrij", left_rows, shard_piece, preferred_element_type=jnp.float32
    )
    piece_stations = shard_piece.shape[1] // 2
    voices = shard_piece.reshape(2, piece_stations, 2, group_count, contraction)
    beam_running = jnp.einsum(
        "obps,pslvk->oblvk", own_beams, voices, preferred_element_type=jnp.float32
    )
    visibilities = columns * vis_scale
    beam_energy = jnp.sum(beam_running * beam_running, axis=(0, 2)).reshape(
        beam_local, group_count, AVG, all_frames
    )
    beam_energy = jnp.sum(beam_energy, axis=3).reshape(beam_local, local_channels) / all_frames
    beam_power = beam_energy.T
    return (visibilities, beam_power)


def phase_table(rows, columns, period):
    products = np.arange(rows)[:, None] * np.arange(columns)[None, :]
    angle = 2.0 * np.pi / period * (products % period)
    return np.cos(angle).astype(np.float32), np.sin(angle).astype(np.float32)


def short_fft(parts):
    count = len(parts)
    if count == 1:
        return parts
    even = short_fft(parts[0::2])
    odd = short_fft(parts[1::2])
    low, high = [], []
    for place in range(count // 2):
        (even_re, even_im), (odd_re, odd_im) = even[place], odd[place]
        if place == 0:
            turn_re, turn_im = odd_re, odd_im
        elif 4 * place == count:
            turn_re, turn_im = odd_im, -odd_re
        else:
            cosine = math.cos(2.0 * math.pi * place / count)
            sine = math.sin(2.0 * math.pi * place / count)
            turn_re = cosine * odd_re + sine * odd_im
            turn_im = cosine * odd_im - sine * odd_re
        low.append((even_re + turn_re, even_im + turn_im))
        high.append((even_re - turn_re, even_im - turn_im))
    return low + high


def swap_octet(blocks):
    lane = lax.broadcasted_iota(jnp.int32, blocks[0].shape, 1)
    width = blocks[0].shape[1]
    for step in (1, 2, 4):
        keep = lane & step == 0
        swapped = list(blocks)
        for low in range(8):
            if low & step == 0:
                high = low + step
                swapped[low] = jnp.where(keep, blocks[low], pltpu.roll(blocks[high], step, 1))
                swapped[high] = jnp.where(keep, pltpu.roll(blocks[low], width - step, 1), blocks[high])
        blocks = swapped
    return blocks


def flip(place, mask, count):
    result, step = 0, 1
    while step < count:
        bit = place // step % 2
        result = result + step * (1 - bit if mask & step else bit)
        step *= 2
    return result


def channelize(half, hooks, refs, scratch):
    rows_ref, coef_ref, gain_ref, twist_cos_ref, twist_sin_ref, w_high_ref, w_low_ref = refs
    received, filt, stage, spec, picked, turned, spectra = scratch
    frames, _, inputs, length = received.shape[1:]
    sections = length // LANES
    hooks = list(hooks)

    def staged(total, pieces, unroll):
        size = total // pieces

        def run(body):
            for piece in range(pieces):
                pl.loop(piece * size, (piece + 1) * size, unroll=unroll)(body)
                if hooks:
                    hooks.pop(0)()

        return run

    @staged(sections, 2, 1)
    def _(section):
        lanes = pl.ds(pl.multiple_of(section * LANES, LANES), LANES)
        taps = [coef_ref[k : k + 1, lanes] for k in range(TAPS)]
        for part in range(2):
            window = []
            for frame in range(frames):
                window = [received[half, frame, part, :, lanes].astype(jnp.float32)] + window[: TAPS - 1]
                total = taps[0] * window[0]
                for k in range(1, len(window)):
                    total = total + taps[k] * window[k]
                filt[section, part, frame] = total

    @staged(frames, 2, 1)
    def _(frame):
        values = [(filt[s, 0, frame], filt[s, 1, frame]) for s in range(sections)]
        row = pl.multiple_of(frame * 8, 8)
        for c, (re, im) in enumerate(short_fft(values)):
            cosine, sine = twist_cos_ref[c : c + 1, :], twist_sin_ref[c : c + 1, :]
            stage[c, pl.ds(row, 8), :LANES] = re * cosine + im * sine
            stage[c, pl.ds(row, 8), LANES:] = im * cosine - re * sine

    over_lanes = (((1,), (1,)), ((), ()))

    @staged(sections, 2, 4)
    def _(c):
        value = stage[c]
        high = value.astype(jnp.bfloat16)
        low = (value - high.astype(jnp.float32)).astype(jnp.bfloat16)
        w_high, w_low = w_high_ref[...], w_low_ref[...]
        result = lax.dot_general(w_high, high, over_lanes, preferred_element_type=jnp.float32)
        result += lax.dot_general(w_high, low, over_lanes, preferred_element_type=jnp.float32)
        result += lax.dot_general(w_low, high, over_lanes, preferred_element_type=jnp.float32)
        result = result * gain_ref[half : half + 1, :]
        place = pl.ds(pl.multiple_of(c * LANES, LANES), LANES)
        spec[place, : frames * inputs] = result[:LANES]
        spec[place, frames * inputs :] = result[LANES:]

    @staged(length // 64, 2, 1)
    def _(step):
        base = pl.multiple_of(step * 64, 64)
        for begin in range(0, 64, 16):
            rows = [spec[pl.ds(rows_ref[base + begin + j], 1), :] for j in range(16)]
            for j, row in enumerate(rows):
                group, place = divmod(begin + j, 8)
                picked[pl.ds(base + place * 8 + group, 1), :] = row

    depth = 2 * inputs

    @staged(length // 64, 2, 2)
    def _(step):
        base = pl.multiple_of(step * 64, 64)
        target = pl.multiple_of(step * (8 * depth), 8 * depth)
        for part in range(2):
            lanes = slice(part * LANES, (part + 1) * LANES)
            blocks = [picked[pl.ds(base + place * 8, 8), lanes] for place in range(8)]
            for i, block in enumerate(swap_octet(blocks)):
                turned[pl.ds(target + part * inputs + i, 8, stride=depth), :] = block

    @staged(length // 64, 1, 4)
    def _(step):
        target = pl.multiple_of(step * (8 * depth), 8 * depth)
        rounded = turned[pl.ds(target, 8 * depth), :].astype(jnp.bfloat16)
        spectra[half, pl.ds(step * 8, 8)] = rounded.reshape(8, depth, LANES)

    for hook in hooks:
        hook()


def beam_rows_into(beam_ref, tables, side, sums):
    stations_ref, weight_re_ref, weight_im_ref = tables
    picks, beam_count = stations_ref.shape
    station_count = sums.shape[1] // 2
    place = lax.broadcasted_iota(jnp.int32, (station_count, beam_count), 0)

    def add(pick, totals):
        hit = place == stations_ref[pl.ds(pick, 1), :]
        return tuple(
            total + jnp.where(hit, ref[pl.ds(pick, 1), :], 0.0)
            for total, ref in zip(totals, (weight_re_ref, weight_im_ref))
        )

    zero = jnp.zeros((station_count, beam_count), jnp.float32)
    total_re, total_im = lax.fori_loop(0, picks, add, (zero, zero))
    sums[:, :station_count] = total_re.T
    sums[:, station_count:] = total_im.T
    own_count = beam_count // 2
    own = sums[pl.ds(pl.multiple_of(side * own_count, own_count), own_count), :].astype(jnp.bfloat16)
    matrix_re, matrix_im = own[:, :station_count], own[:, station_count:]
    inputs = 2 * station_count
    station = lax.broadcasted_iota(jnp.int32, (station_count, inputs), 0)
    column = lax.broadcasted_iota(jnp.int32, (station_count, inputs), 1)
    for polarization in range(2):
        spread = (column == 2 * station + polarization).astype(jnp.bfloat16)
        wide_re = jnp.dot(matrix_re, spread, preferred_element_type=jnp.float32)
        wide_im = jnp.dot(matrix_im, spread, preferred_element_type=jnp.float32)
        rows = pl.ds(polarization * own_count, own_count)
        beam_ref[rows, :inputs] = wide_re.astype(jnp.bfloat16)
        beam_ref[rows, inputs:] = (-wide_im).astype(jnp.bfloat16)
        rows = pl.ds((2 + polarization) * own_count, own_count)
        beam_ref[rows, :inputs] = wide_im.astype(jnp.bfloat16)
        beam_ref[rows, inputs:] = wide_re.astype(jnp.bfloat16)


def gain_into(gain, flags_ref, first):
    inputs = gain.shape[1] // 2
    pair = lax.broadcasted_iota(jnp.int32, (1, LANES), 1) % 8 // 2
    for half in range(2):
        row = jnp.zeros((1, LANES), jnp.int32)
        for k in range(4):
            row = jnp.where(pair == k, flags_ref[first + half * 4 + k], row)
        gain[half : half + 1, :] = row.astype(jnp.float32)


def rows_into(rows_ref, order_ref, sections):
    shift = sections.bit_length() - 1

    @pl.loop(0, order_ref.shape[0] // 16)
    def _(step):
        for j in range(16):
            channel = order_ref[step * 16 + j]
            rows_ref[step * 16 + j] = (channel & (sections - 1)) * LANES + (channel >> shift)


def turn_kernel(
    count, near_count, split, flights, early,
    order_ref, flags_ref, volt_ref, stations_ref, weight_re_ref, weight_im_ref,
    coef_ref, twist_cos_ref, twist_sin_ref, w_high_ref, w_low_ref,
    out_ref, beam_ref,
    rows_ref, gain_ref, sums, received, filt, stage, spec, picked, turned, spectra,
    hold, in_local, in_send, in_recv, out_local, out_send, out_recv, cross_send, cross_recv,
):
    me, side = lax.axis_index("wide"), lax.axis_index("narrow")
    mesh_ids = pl.DeviceIdType.MESH
    groups = spectra.shape[1] // count
    inputs = received.shape[3]
    barrier = pltpu.get_barrier_semaphore()
    for mask in range(1, count):
        pl.semaphore_signal(barrier, inc=1, device_id={"wide": flip(me, mask, count)}, device_id_type=mesh_ids)
    for mask in range(near_count):
        target = {"wide": flip(me, mask, count), "narrow": 1 - side}
        pl.semaphore_signal(barrier, inc=1, device_id=target, device_id_type=mesh_ids)
    pl.semaphore_wait(barrier, count - 1 + near_count)

    def entering(half, mask, back=False):
        peer = flip(me, mask, count)
        return pltpu.make_async_remote_copy(
            src_ref=volt_ref.at[:, peer, half],
            dst_ref=received.at[half, peer if back else me],
            send_sem=in_send.at[half, mask],
            recv_sem=in_recv.at[half, mask],
            device_id={"wide": peer},
            device_id_type=mesh_ids,
        )

    def kept_in(half):
        return pltpu.make_async_copy(volt_ref.at[:, me, half], received.at[half, me], in_local.at[half])

    def kept_out(half):
        return pltpu.make_async_copy(
            spectra.at[half, pl.ds(me * groups, groups)], out_ref.at[side, me, half], out_local.at[half]
        )

    def rows_of(half, mask, piece):
        size = groups // (split[half] if mask >= near_count else 1)
        return piece * size, size

    def outgoing(half, item, back=False):
        mask, piece = item
        begin, size = rows_of(half, mask, piece)
        peer = flip(me, mask, count)
        return pltpu.make_async_remote_copy(
            src_ref=spectra.at[half, pl.ds(peer * groups + begin, size)],
            dst_ref=out_ref.at[side, peer if back else me, half, pl.ds(begin, size)],
            send_sem=out_send.at[half, piece, mask],
            recv_sem=out_recv.at[half, piece, mask],
            device_id={"wide": peer},
            device_id_type=mesh_ids,
        )

    def across(half, item, back=False):
        mask, piece = item
        begin, size = rows_of(half, mask, piece)
        peer = flip(me, mask, count)
        place = pl.ds(begin, size)
        target_side = 1 - side if back else side
        if mask < near_count:
            source = spectra.at[half, pl.ds(peer * groups, groups)]
            target = out_ref.at[target_side, peer if back else me, half, place]
            device = {"wide": peer, "narrow": 1 - side}
        else:
            source = out_ref.at[side, peer, half, place]
            target = out_ref.at[target_side, peer, half, place]
            device = {"narrow": 1 - side}
        return pltpu.make_async_remote_copy(
            src_ref=source,
            dst_ref=target,
            send_sem=cross_send.at[half, piece, mask],
            recv_sem=cross_recv.at[half, piece, mask],
            device_id=device,
            device_id_type=mesh_ids,
        )

    near = [(mask, 0) for mask in range(1, near_count)]
    later = list(range(near_count, count // 2)) + list(range(count // 2, count))
    orders = [[(mask, piece) for mask in later for piece in range(split[half])] for half in range(2)]
    entry = list(range(count // 2, count)) + list(range(1, count // 2))
    refs = (rows_ref, coef_ref, gain_ref, twist_cos_ref, twist_sin_ref, w_high_ref, w_low_ref)
    scratch = (received, filt, stage, spec, picked, turned, spectra)

    def leave(half):
        for item in orders[half][: flights[half]]:
            outgoing(half, item).start()
        for item in near:
            outgoing(half, item).start()
        for item in [(0, 0)] + near:
            across(half, item).start()
        kept_out(half).start()

    def pass_on(half, place):
        def step():
            order = orders[half]
            if place + flights[half] < len(order):
                outgoing(half, order[place]).wait_send()
                outgoing(half, order[place + flights[half]]).start()
            outgoing(half, order[place], True).wait_recv()
            across(half, order[place]).start()

        return step

    for mask in entry:
        entering(0, mask).start()
    for half in range(2):
        kept_in(half).start()
    beam_rows_into(beam_ref, (stations_ref, weight_re_ref, weight_im_ref), side, sums)
    gain_into(gain_ref, flags_ref, (side * count + me) * inputs)
    rows_into(rows_ref, order_ref, twist_cos_ref.shape[0])
    for mask in entry:
        entering(0, mask).wait_send()
    for mask in entry[:early]:
        entering(1, mask).start()
    for mask in entry:
        entering(0, mask, True).wait_recv()
    neighbour = {"wide": flip(me, count // 4, count)}
    pl.semaphore_signal(hold, inc=1, device_id=neighbour, device_id_type=mesh_ids)
    pl.semaphore_wait(hold, 1)
    for mask in entry[early:]:
        entering(1, mask).start()
    kept_in(0).wait()
    channelize(0, [], refs, scratch)
    leave(0)
    kept_in(1).wait()
    for mask in entry:
        entering(1, mask).wait_send()
    for mask in entry:
        entering(1, mask, True).wait_recv()
    channelize(1, [pass_on(0, place) for place in range(len(orders[0]))], refs, scratch)
    leave(1)
    for place in range(len(orders[1])):
        pass_on(1, place)()
    for half in range(2):
        kept_out(half).wait()
        for item in near:
            outgoing(half, item).wait_send()
            outgoing(half, item, True).wait_recv()
        for item in orders[half][max(0, len(orders[half]) - flights[half]) :]:
            outgoing(half, item).wait_send()
        for item in [(0, 0)] + near + orders[half]:
            across(half, item).wait_send()
            across(half, item, True).wait_recv()


def turn(voltages, order, flags, tables, coefficients, near_count=4, split=(1, 1), flights=(6, 4), early=2):
    _, count, halves, inputs, length = voltages.shape
    sections = length // LANES
    twist_cos, twist_sin = phase_table(sections, LANES, length)
    cosine, sine = phase_table(LANES, LANES, LANES)
    weights = np.concatenate(
        [np.concatenate([cosine, sine], axis=1), np.concatenate([-sine, cosine], axis=1)], axis=0
    ) / np.float32(math.sqrt(length))
    w_high = weights.astype(jnp.bfloat16)
    w_low = (weights - w_high.astype(np.float32)).astype(jnp.bfloat16)
    scalars = pl.BlockSpec(memory_space=pltpu.SMEM)
    whole = pl.BlockSpec(memory_space=pltpu.VMEM)
    anywhere = pl.BlockSpec(memory_space=pltpu.HBM)
    depth = 2 * inputs
    beam_count, station_count = tables[0].shape[1], flags.shape[0]
    pair = pltpu.SemaphoreType.DMA((halves,))
    table = pltpu.SemaphoreType.DMA((halves, count))
    pieces = pltpu.SemaphoreType.DMA((halves, max(split), count))
    return pl.pallas_call(
        functools.partial(turn_kernel, count, near_count, split, flights, early),
        out_shape=(
            jax.ShapeDtypeStruct((2, count, halves, length // AVG // count, depth, LANES), jnp.bfloat16),
            jax.ShapeDtypeStruct((2 * beam_count, 4 * station_count), jnp.bfloat16),
        ),
        in_specs=[scalars, scalars, anywhere] + [whole] * 8,
        out_specs=(pl.BlockSpec(memory_space=pl.ANY), whole),
        scratch_shapes=[
            pltpu.SMEM((length,), jnp.int32),
            pltpu.VMEM((halves, LANES), jnp.float32),
            pltpu.VMEM((beam_count, 2 * station_count), jnp.float32),
            pltpu.VMEM((halves, count, 2, inputs, length), jnp.bfloat16),
            pltpu.VMEM((sections, 2, count, inputs, LANES), jnp.float32),
            pltpu.VMEM((sections, count * inputs, 2 * LANES), jnp.float32),
            pltpu.VMEM((length, 2 * count * inputs), jnp.float32),
            pltpu.VMEM((length, 2 * count * inputs), jnp.float32),
            pltpu.VMEM((length // 8 * depth, LANES), jnp.float32),
            pltpu.VMEM((halves, length // 8, depth, LANES), jnp.bfloat16),
            pltpu.SemaphoreType.REGULAR,
            pair, table, table, pair, pieces, pieces, pieces, pieces,
        ],
        compiler_params=pltpu.CompilerParams(
            collective_id=0, has_side_effects=True, vmem_limit_bytes=60 * 2**20
        ),
        name="turn",
    )(order, flags, voltages, *tables, coefficients, twist_cos, twist_sin, jnp.asarray(w_high), jnp.asarray(w_low))


def parts_of(block):
    rows = block.reshape(-1, 16, LANES).astype(jnp.float32)
    return [
        rows[:, begin : begin + 8].reshape(-1, LANES).astype(jnp.bfloat16) for begin in (0, 8)
    ]


def correlate_kernel(scale, frame_count, side_ref, all_ref, beam_ref, vis_ref, power_ref):
    over_lanes = (((1,), (1,)), ((), ()))
    count = power_ref.shape[0]
    batch = vis_ref.shape[0]
    step = pl.program_id(0)
    stacked = []
    for group in range(batch):
        own_re, own_im = parts_of(all_ref[side_ref[0], :, :, group])
        re, im = parts_of(all_ref[:, :, :, group])
        both = jnp.concatenate([re, im], axis=1)
        left_re = jnp.concatenate([own_re, own_im], axis=1)
        left_im = jnp.concatenate([own_im, -own_re], axis=1)
        vis_ref[group, 0] = scale * lax.dot_general(
            left_re, both, over_lanes, preferred_element_type=jnp.float32
        )
        vis_ref[group, 1] = scale * lax.dot_general(
            left_im, both, over_lanes, preferred_element_type=jnp.float32
        )
        stacked.append(jnp.concatenate([re, im], axis=0))
    beam = jnp.dot(
        beam_ref[...], jnp.concatenate(stacked, axis=1), preferred_element_type=jnp.float32
    )
    energy = beam * beam
    total = energy[:count]
    for piece in range(1, energy.shape[0] // count):
        total = total + energy[piece * count : (piece + 1) * count]
    lane = lax.broadcasted_iota(jnp.int32, (count, LANES), 1)
    tiles = LANES // AVG // batch
    lanes = pl.ds(pl.multiple_of(step // tiles * LANES, LANES), LANES)
    merged = power_ref[:, lanes]
    for group in range(batch):
        part = total[:, group * LANES : (group + 1) * LANES]
        shift = AVG
        while shift < LANES:
            part = part + pltpu.roll(part, shift, 1)
            shift *= 2
        merged = jnp.where(lane // AVG == step % tiles * batch + group, part / frame_count, merged)
    power_ref[:, lanes] = merged


def correlate(gathered, side, beam_rows, frame_count):
    sides, sources, halves, groups, depth, _ = gathered.shape
    rows = sources * halves * 8
    batch = math.gcd(groups, 4)
    beam_local = beam_rows.shape[0] // 4
    return pl.pallas_call(
        functools.partial(correlate_kernel, 1.0 / math.sqrt(AVG * frame_count), frame_count),
        grid_spec=pltpu.PrefetchScalarGridSpec(
            num_scalar_prefetch=1,
            grid=(groups // batch,),
            in_specs=[
                pl.BlockSpec((sides, sources, halves, batch, depth, LANES), lambda v, at: (0, 0, 0, v, 0, 0)),
                pl.BlockSpec(beam_rows.shape, lambda v, at: (0, 0)),
            ],
            out_specs=(
                pl.BlockSpec((batch, 2, rows, sides * rows), lambda v, at: (v, 0, 0, 0)),
                pl.BlockSpec((beam_local, groups * AVG), lambda v, at: (0, 0)),
            ),
        ),
        out_shape=(
            jax.ShapeDtypeStruct((groups, 2, rows, sides * rows), jnp.float32),
            jax.ShapeDtypeStruct((beam_local, groups * AVG), jnp.float32),
        ),
        compiler_params=pltpu.CompilerParams(vmem_limit_bytes=60 * 2**20),
        name="correlate",
    )(side.reshape(1), gathered, beam_rows)


def fast_shards(voltages, station_flags, channel_order, beam_stations, beam_weight_re, beam_weight_im):
    local_inputs, frames, length = voltages.shape[1:]
    devices = lax.axis_size("wide")
    blocks = voltages.reshape(2, devices, 2, local_inputs // devices // 2, length)
    tables = [table.T for table in (beam_stations, beam_weight_re, beam_weight_im)]
    gathered, beam_rows = turn(blocks, channel_order, station_flags, tables, prototype(TAPS, length))
    visibilities, power = correlate(gathered, lax.axis_index("narrow"), beam_rows, devices * frames)
    return visibilities, power.T


def solution(mesh):
    def body(*args):
        local_inputs, frames, length = args[0].shape[1:]
        devices = mesh.shape["wide"]
        share = local_inputs // devices
        sections = length // LANES
        fits = (
            frames == 1
            and local_inputs % devices == 0
            and share == 16
            and mesh.shape["narrow"] == 2
            and devices * AVG == LANES
            and length % (LANES * devices) == 0
            and args[3].shape[0] % 32 == 0
            and args[1].shape[0] == local_inputs
            and sections & (sections - 1) == 0
        )
        return (fast_shards if fits else shards)(*args)

    return jax.shard_map(
        body,
        mesh=mesh,
        in_specs=(P(None, "narrow", "wide", None), P(), P(), P(), P(), P()),
        out_specs=(P("wide", None, "narrow", None), P("wide", "narrow")),
        check_vma=False,
    )
```

```python
import functools
import math

import jax
import jax.numpy as jnp
import numpy as np
from jax import lax
from jax.experimental import pallas as pl
from jax.experimental.pallas import tpu as pltpu
from jax.sharding import PartitionSpec as P

TAPS = 8
AVG = 8
LANES = 128


def prototype(tap_count, length):
    places = np.arange(tap_count * length)
    offsets = places / length - tap_count / 2.0
    window = 0.5 - 0.5 * np.cos(2.0 * np.pi * (places + 0.5) / (tap_count * length))
    return (np.sinc(offsets) * window).astype(np.float32).reshape(tap_count, length)


def dense_weights(selection, weight_re, weight_im, station_count):
    beam_count, pick_count = selection.shape
    beam_rows = lax.broadcasted_iota(jnp.int32, (beam_count, pick_count), 0)
    flat_index = (beam_rows * station_count + selection).reshape(-1)
    summed_re = jax.ops.segment_sum(
        weight_re.reshape(-1), flat_index, num_segments=beam_count * station_count
    )
    summed_im = jax.ops.segment_sum(
        weight_im.reshape(-1), flat_index, num_segments=beam_count * station_count
    )
    return (
        summed_re.reshape(beam_count, station_count).astype(jnp.bfloat16),
        summed_im.reshape(beam_count, station_count).astype(jnp.bfloat16),
    )


def transform(filtered):
    input_count, frame_count, length = (filtered.shape[1], filtered.shape[2], filtered.shape[3])
    section_size = math.isqrt(length)
    counter = jnp.arange(section_size, dtype=jnp.int32)
    products = counter[:, None] * counter[None, :]
    section_angle = 2.0 * math.pi / section_size * (products % section_size).astype(jnp.float32)
    twist_angle = 2.0 * math.pi / length * products.astype(jnp.float32)
    cosine = jnp.cos(section_angle)
    sine_table = jnp.sin(section_angle)
    twist_cos = jnp.cos(twist_angle)
    twist_sin = jnp.sin(twist_angle)
    mixing = jnp.concatenate(
        [
            jnp.concatenate([cosine, -sine_table], axis=1),
            jnp.concatenate([sine_table, cosine], axis=1),
        ],
        axis=0,
    )
    twist_scale = jnp.concatenate([twist_cos, twist_cos], axis=1)
    twist_cross = jnp.concatenate([twist_sin, -twist_sin], axis=1)
    sample_grid = filtered.reshape(2, input_count, frame_count, section_size, section_size)
    stacked = jnp.moveaxis(sample_grid, 0, 3).reshape(
        input_count, frame_count, section_size, 2 * section_size
    )
    first_pass = jnp.einsum("cn,ifnk->ifck", cosine, stacked, precision=lax.Precision.HIGHEST)
    second_pass = jnp.einsum("cn,ifnk->ifck", sine_table, stacked, precision=lax.Precision.HIGHEST)
    sectioned = first_pass + jnp.concatenate(
        [second_pass[..., section_size:], -second_pass[..., :section_size]], axis=-1
    )
    swapped = jnp.concatenate(
        [sectioned[..., section_size:], sectioned[..., :section_size]], axis=-1
    )
    twisted = sectioned * twist_scale + swapped * twist_cross
    result = jnp.einsum("ifck,kj->ifcj", twisted, mixing, precision=lax.Precision.HIGHEST)
    return result * (1.0 / math.sqrt(length))


def row_stack(grouped):
    part_re, part_im = (grouped[0], grouped[1])
    return jnp.stack(
        [jnp.stack([part_re, part_im], axis=2), jnp.stack([part_im, -part_re], axis=2)], axis=0
    )


def apply_taps_long(extended, coefficients, frame_count):
    result = jnp.zeros(extended.shape[:2] + (frame_count, extended.shape[3]), jnp.float32)
    for tap_index in range(TAPS):
        begin = TAPS - 1 - tap_index
        result = result + coefficients[tap_index] * extended[
            :, :, begin : begin + frame_count
        ].astype(jnp.float32)
    return result


def shards(voltages, station_flags, channel_order, beam_stations, beam_weight_re, beam_weight_im):
    local_inputs = voltages.shape[1]
    frame_count = voltages.shape[2]
    length = voltages.shape[3]
    section_size = math.isqrt(length)
    coefficients = prototype(TAPS, length)
    across = lax.all_to_all(voltages, "wide", split_axis=3, concat_axis=2, tiled=True)
    column_count = across.shape[3]
    total_frames = across.shape[2]
    own_coeffs = lax.dynamic_slice_in_dim(
        coefficients, lax.axis_index("wide") * column_count, column_count, axis=1
    )
    padded = jnp.pad(across, ((0, 0), (0, 0), (TAPS - 1, 0), (0, 0)))
    local_filtered = apply_taps_long(padded, own_coeffs, total_frames)
    filtered = lax.all_to_all(local_filtered, "wide", split_axis=2, concat_axis=3, tiled=True)
    spectrum = transform(filtered)
    layout = spectrum.reshape(local_inputs, frame_count, section_size, 2, section_size)
    layout = jnp.transpose(layout, (3, 0, 2, 4, 1)).reshape(2, local_inputs, length, frame_count)
    local_stations = local_inputs // 2
    own_flags = lax.dynamic_slice_in_dim(
        station_flags, lax.axis_index("narrow") * local_stations, local_stations
    )
    input_gain = jnp.repeat(own_flags, 2).astype(jnp.float32)
    rounded = (layout * input_gain[None, :, None, None]).astype(jnp.bfloat16)
    position = channel_order % section_size * section_size + channel_order // section_size
    chosen = (position[:, None] == jnp.arange(length)[None, :]).astype(jnp.bfloat16)
    spectra = jnp.einsum('pk,rikf->ripf', chosen, rounded)
    turned = lax.all_to_all(spectra, "wide", split_axis=2, concat_axis=3, tiled=True)
    local_channels = turned.shape[2]
    all_frames = turned.shape[3]
    group_count = local_channels // AVG
    contraction = AVG * all_frames
    grouped = turned.reshape(2, local_inputs, group_count, contraction)
    vis_scale = 1.0 / math.sqrt(contraction)
    matrix_re, matrix_im = dense_weights(
        beam_stations, beam_weight_re, beam_weight_im, station_flags.shape[0]
    )
    beam_block = jnp.stack(
        [jnp.stack([matrix_re, -matrix_im], axis=1), jnp.stack([matrix_im, matrix_re], axis=1)],
        axis=0,
    )
    narrow_count = lax.axis_size("narrow")
    beam_local = beam_block.shape[1] // narrow_count
    own_beams = lax.dynamic_slice_in_dim(
        beam_block, lax.axis_index("narrow") * beam_local, beam_local, axis=1
    )
    left_rows = row_stack(grouped)
    shard_piece = lax.all_gather(grouped, "narrow", axis=1, tiled=True)
    columns = jnp.einsum(
        "rivqk,qjvk->vrij", left_rows, shard_piece, preferred_element_type=jnp.float32
    )
    piece_stations = shard_piece.shape[1] // 2
    voices = shard_piece.reshape(2, piece_stations, 2, group_count, contraction)
    beam_running = jnp.einsum(
        "obps,pslvk->oblvk", own_beams, voices, preferred_element_type=jnp.float32
    )
    visibilities = columns * vis_scale
    beam_energy = jnp.sum(beam_running * beam_running, axis=(0, 2)).reshape(
        beam_local, group_count, AVG, all_frames
    )
    beam_energy = jnp.sum(beam_energy, axis=3).reshape(beam_local, local_channels) / all_frames
    beam_power = beam_energy.T
    return (visibilities, beam_power)


def phase_table(rows, columns, period):
    products = np.arange(rows)[:, None] * np.arange(columns)[None, :]
    angle = 2.0 * np.pi / period * (products % period)
    return np.cos(angle).astype(np.float32), np.sin(angle).astype(np.float32)


def short_fft(parts):
    count = len(parts)
    if count == 1:
        return parts
    even = short_fft(parts[0::2])
    odd = short_fft(parts[1::2])
    low, high = [], []
    for place in range(count // 2):
        (even_re, even_im), (odd_re, odd_im) = even[place], odd[place]
        if place == 0:
            turn_re, turn_im = odd_re, odd_im
        elif 4 * place == count:
            turn_re, turn_im = odd_im, -odd_re
        else:
            cosine = math.cos(2.0 * math.pi * place / count)
            sine = math.sin(2.0 * math.pi * place / count)
            turn_re = cosine * odd_re + sine * odd_im
            turn_im = cosine * odd_im - sine * odd_re
        low.append((even_re + turn_re, even_im + turn_im))
        high.append((even_re - turn_re, even_im - turn_im))
    return low + high


def swap_octet(blocks):
    lane = lax.broadcasted_iota(jnp.int32, blocks[0].shape, 1)
    width = blocks[0].shape[1]
    for step in (1, 2, 4):
        keep = lane & step == 0
        swapped = list(blocks)
        for low in range(8):
            if low & step == 0:
                high = low + step
                swapped[low] = jnp.where(keep, blocks[low], pltpu.roll(blocks[high], step, 1))
                swapped[high] = jnp.where(keep, pltpu.roll(blocks[low], width - step, 1), blocks[high])
        blocks = swapped
    return blocks


def flip(place, mask, count):
    result, step = 0, 1
    while step < count:
        bit = place // step % 2
        result = result + step * (1 - bit if mask & step else bit)
        step *= 2
    return result


def channelize(half, hooks, refs, scratch):
    rows_ref, coef_ref, gain_ref, twist_cos_ref, twist_sin_ref, w_high_ref, w_low_ref = refs
    received, filt, stage, spec, picked, turned, spectra = scratch
    frames, _, inputs, length = received.shape[1:]
    sections = length // LANES
    hooks = list(hooks)

    def staged(total, pieces, unroll):
        size = total // pieces

        def run(body):
            for piece in range(pieces):
                pl.loop(piece * size, (piece + 1) * size, unroll=unroll)(body)
                if hooks:
                    hooks.pop(0)()

        return run

    @staged(sections, 2, 1)
    def _(section):
        lanes = pl.ds(pl.multiple_of(section * LANES, LANES), LANES)
        taps = [coef_ref[k : k + 1, lanes] for k in range(TAPS)]
        for part in range(2):
            window = []
            for frame in range(frames):
                window = [received[half, frame, part, :, lanes].astype(jnp.float32)] + window[: TAPS - 1]
                total = taps[0] * window[0]
                for k in range(1, len(window)):
                    total = total + taps[k] * window[k]
                filt[section, part, frame] = total

    @staged(frames, 2, 1)
    def _(frame):
        values = [(filt[s, 0, frame], filt[s, 1, frame]) for s in range(sections)]
        row = pl.multiple_of(frame * 8, 8)
        for c, (re, im) in enumerate(short_fft(values)):
            cosine, sine = twist_cos_ref[c : c + 1, :], twist_sin_ref[c : c + 1, :]
            stage[c, pl.ds(row, 8), :LANES] = re * cosine + im * sine
            stage[c, pl.ds(row, 8), LANES:] = im * cosine - re * sine

    over_lanes = (((1,), (1,)), ((), ()))

    @staged(sections, 2, 4)
    def _(c):
        value = stage[c]
        high = value.astype(jnp.bfloat16)
        low = (value - high.astype(jnp.float32)).astype(jnp.bfloat16)
        w_high, w_low = w_high_ref[...], w_low_ref[...]
        result = lax.dot_general(w_high, high, over_lanes, preferred_element_type=jnp.float32)
        result += lax.dot_general(w_high, low, over_lanes, preferred_element_type=jnp.float32)
        result += lax.dot_general(w_low, high, over_lanes, preferred_element_type=jnp.float32)
        result = result * gain_ref[half : half + 1, :]
        place = pl.ds(pl.multiple_of(c * LANES, LANES), LANES)
        spec[place, : frames * inputs] = result[:LANES]
        spec[place, frames * inputs :] = result[LANES:]

    @staged(length // 64, 2, 1)
    def _(step):
        base = pl.multiple_of(step * 64, 64)
        for begin in range(0, 64, 16):
            rows = [spec[pl.ds(rows_ref[base + begin + j], 1), :] for j in range(16)]
            for j, row in enumerate(rows):
                group, place = divmod(begin + j, 8)
                picked[pl.ds(base + place * 8 + group, 1), :] = row

    depth = 2 * inputs

    @staged(length // 64, 2, 2)
    def _(step):
        base = pl.multiple_of(step * 64, 64)
        target = pl.multiple_of(step * (8 * depth), 8 * depth)
        for part in range(2):
            lanes = slice(part * LANES, (part + 1) * LANES)
            blocks = [picked[pl.ds(base + place * 8, 8), lanes] for place in range(8)]
            for i, block in enumerate(swap_octet(blocks)):
                turned[pl.ds(target + part * inputs + i, 8, stride=depth), :] = block

    @staged(length // 64, 1, 4)
    def _(step):
        target = pl.multiple_of(step * (8 * depth), 8 * depth)
        rounded = turned[pl.ds(target, 8 * depth), :].astype(jnp.bfloat16)
        spectra[half, pl.ds(step * 8, 8)] = rounded.reshape(8, depth, LANES)

    for hook in hooks:
        hook()


def beam_rows_into(beam_ref, tables, side, sums):
    stations_ref, weight_re_ref, weight_im_ref = tables
    picks, beam_count = stations_ref.shape
    station_count = sums.shape[1] // 2
    place = lax.broadcasted_iota(jnp.int32, (station_count, beam_count), 0)

    def add(pick, totals):
        hit = place == stations_ref[pl.ds(pick, 1), :]
        return tuple(
            total + jnp.where(hit, ref[pl.ds(pick, 1), :], 0.0)
            for total, ref in zip(totals, (weight_re_ref, weight_im_ref))
        )

    zero = jnp.zeros((station_count, beam_count), jnp.float32)
    total_re, total_im = lax.fori_loop(0, picks, add, (zero, zero))
    sums[:, :station_count] = total_re.T
    sums[:, station_count:] = total_im.T
    own_count = beam_count // 2
    own = sums[pl.ds(pl.multiple_of(side * own_count, own_count), own_count), :].astype(jnp.bfloat16)
    matrix_re, matrix_im = own[:, :station_count], own[:, station_count:]
    inputs = 2 * station_count
    station = lax.broadcasted_iota(jnp.int32, (station_count, inputs), 0)
    column = lax.broadcasted_iota(jnp.int32, (station_count, inputs), 1)
    for polarization in range(2):
        spread = (column == 2 * station + polarization).astype(jnp.bfloat16)
        wide_re = jnp.dot(matrix_re, spread, preferred_element_type=jnp.float32)
        wide_im = jnp.dot(matrix_im, spread, preferred_element_type=jnp.float32)
        rows = pl.ds(polarization * own_count, own_count)
        beam_ref[rows, :inputs] = wide_re.astype(jnp.bfloat16)
        beam_ref[rows, inputs:] = (-wide_im).astype(jnp.bfloat16)
        rows = pl.ds((2 + polarization) * own_count, own_count)
        beam_ref[rows, :inputs] = wide_im.astype(jnp.bfloat16)
        beam_ref[rows, inputs:] = wide_re.astype(jnp.bfloat16)


def gain_into(gain, flags_ref, first):
    inputs = gain.shape[1] // 2
    pair = lax.broadcasted_iota(jnp.int32, (1, LANES), 1) % 8 // 2
    for half in range(2):
        row = jnp.zeros((1, LANES), jnp.int32)
        for k in range(4):
            row = jnp.where(pair == k, flags_ref[first + half * 4 + k], row)
        gain[half : half + 1, :] = row.astype(jnp.float32)


def rows_into(rows_ref, order_ref, sections):
    shift = sections.bit_length() - 1

    @pl.loop(0, order_ref.shape[0] // 16)
    def _(step):
        for j in range(16):
            channel = order_ref[step * 16 + j]
            rows_ref[step * 16 + j] = (channel & (sections - 1)) * LANES + (channel >> shift)


def turn_kernel(
    count, near_count, split, flights, early,
    order_ref, flags_ref, volt_ref, stations_ref, weight_re_ref, weight_im_ref,
    coef_ref, twist_cos_ref, twist_sin_ref, w_high_ref, w_low_ref,
    out_ref, beam_ref,
    rows_ref, gain_ref, sums, received, filt, stage, spec, picked, turned, spectra,
    hold, in_local, in_send, in_recv, out_local, out_send, out_recv, cross_send, cross_recv,
):
    me, side = lax.axis_index("wide"), lax.axis_index("narrow")
    mesh_ids = pl.DeviceIdType.MESH
    groups = spectra.shape[1] // count
    inputs = received.shape[3]
    barrier = pltpu.get_barrier_semaphore()
    for mask in range(1, count):
        pl.semaphore_signal(barrier, inc=1, device_id={"wide": flip(me, mask, count)}, device_id_type=mesh_ids)
    for mask in range(near_count):
        target = {"wide": flip(me, mask, count), "narrow": 1 - side}
        pl.semaphore_signal(barrier, inc=1, device_id=target, device_id_type=mesh_ids)
    pl.semaphore_wait(barrier, count - 1 + near_count)

    def entering(half, mask, back=False):
        peer = flip(me, mask, count)
        return pltpu.make_async_remote_copy(
            src_ref=volt_ref.at[:, peer, half],
            dst_ref=received.at[half, peer if back else me],
            send_sem=in_send.at[half, mask],
            recv_sem=in_recv.at[half, mask],
            device_id={"wide": peer},
            device_id_type=mesh_ids,
        )

    def kept_in(half):
        return pltpu.make_async_copy(volt_ref.at[:, me, half], received.at[half, me], in_local.at[half])

    def kept_out(half):
        return pltpu.make_async_copy(
            spectra.at[half, pl.ds(me * groups, groups)], out_ref.at[side, me, half], out_local.at[half]
        )

    def rows_of(half, mask, piece):
        size = groups // (split[half] if mask >= near_count else 1)
        return piece * size, size

    def outgoing(half, item, back=False):
        mask, piece = item
        begin, size = rows_of(half, mask, piece)
        peer = flip(me, mask, count)
        return pltpu.make_async_remote_copy(
            src_ref=spectra.at[half, pl.ds(peer * groups + begin, size)],
            dst_ref=out_ref.at[side, peer if back else me, half, pl.ds(begin, size)],
            send_sem=out_send.at[half, piece, mask],
            recv_sem=out_recv.at[half, piece, mask],
            device_id={"wide": peer},
            device_id_type=mesh_ids,
        )

    def across(half, item, back=False):
        mask, piece = item
        begin, size = rows_of(half, mask, piece)
        peer = flip(me, mask, count)
        place = pl.ds(begin, size)
        target_side = 1 - side if back else side
        if mask < near_count:
            source = spectra.at[half, pl.ds(peer * groups, groups)]
            target = out_ref.at[target_side, peer if back else me, half, place]
            device = {"wide": peer, "narrow": 1 - side}
        else:
            source = out_ref.at[side, peer, half, place]
            target = out_ref.at[target_side, peer, half, place]
            device = {"narrow": 1 - side}
        return pltpu.make_async_remote_copy(
            src_ref=source,
            dst_ref=target,
            send_sem=cross_send.at[half, piece, mask],
            recv_sem=cross_recv.at[half, piece, mask],
            device_id=device,
            device_id_type=mesh_ids,
        )

    near = [(mask, 0) for mask in range(1, near_count)]
    later = list(range(near_count, count // 2)) + list(range(count // 2, count))
    orders = [[(mask, piece) for mask in later for piece in range(split[half])] for half in range(2)]
    entry = list(range(count // 2, count)) + list(range(1, count // 2))
    refs = (rows_ref, coef_ref, gain_ref, twist_cos_ref, twist_sin_ref, w_high_ref, w_low_ref)
    scratch = (received, filt, stage, spec, picked, turned, spectra)

    def leave(half):
        for item in orders[half][: flights[half]]:
            outgoing(half, item).start()
        for item in near:
            outgoing(half, item).start()
        for item in [(0, 0)] + near:
            across(half, item).start()
        kept_out(half).start()

    def pass_on(half, place):
        def step():
            order = orders[half]
            if place + flights[half] < len(order):
                outgoing(half, order[place]).wait_send()
                outgoing(half, order[place + flights[half]]).start()
            outgoing(half, order[place], True).wait_recv()
            across(half, order[place]).start()

        return step

    for mask in entry:
        entering(0, mask).start()
    for half in range(2):
        kept_in(half).start()
    beam_rows_into(beam_ref, (stations_ref, weight_re_ref, weight_im_ref), side, sums)
    gain_into(gain_ref, flags_ref, (side * count + me) * inputs)
    rows_into(rows_ref, order_ref, twist_cos_ref.shape[0])
    for mask in entry:
        entering(0, mask).wait_send()
    for mask in entry[:early]:
        entering(1, mask).start()
    for mask in entry:
        entering(0, mask, True).wait_recv()
    neighbour = {"wide": flip(me, count // 4, count)}
    pl.semaphore_signal(hold, inc=1, device_id=neighbour, device_id_type=mesh_ids)
    pl.semaphore_wait(hold, 1)
    for mask in entry[early:]:
        entering(1, mask).start()
    kept_in(0).wait()
    channelize(0, [], refs, scratch)
    leave(0)
    kept_in(1).wait()
    for mask in entry:
        entering(1, mask).wait_send()
    for mask in entry:
        entering(1, mask, True).wait_recv()
    forwards = [pass_on(0, place) for place in range(len(orders[0]))]
    beside = [lambda: None] * 3 + forwards[:8]
    channelize(1, beside, refs, scratch)
    leave(1)
    for forward in forwards[8:]:
        forward()
    for place in range(len(orders[1])):
        pass_on(1, place)()
    for half in range(2):
        kept_out(half).wait()
        for item in near:
            outgoing(half, item).wait_send()
            outgoing(half, item, True).wait_recv()
        for item in orders[half][max(0, len(orders[half]) - flights[half]) :]:
            outgoing(half, item).wait_send()
        for item in [(0, 0)] + near + orders[half]:
            across(half, item).wait_send()
            across(half, item, True).wait_recv()


def turn(voltages, order, flags, tables, coefficients, near_count=4, split=(1, 1), flights=(8, 4), early=2):
    _, count, halves, inputs, length = voltages.shape
    sections = length // LANES
    twist_cos, twist_sin = phase_table(sections, LANES, length)
    cosine, sine = phase_table(LANES, LANES, LANES)
    weights = np.concatenate(
        [np.concatenate([cosine, sine], axis=1), np.concatenate([-sine, cosine], axis=1)], axis=0
    ) / np.float32(math.sqrt(length))
    w_high = weights.astype(jnp.bfloat16)
    w_low = (weights - w_high.astype(np.float32)).astype(jnp.bfloat16)
    scalars = pl.BlockSpec(memory_space=pltpu.SMEM)
    whole = pl.BlockSpec(memory_space=pltpu.VMEM)
    anywhere = pl.BlockSpec(memory_space=pltpu.HBM)
    depth = 2 * inputs
    beam_count, station_count = tables[0].shape[1], flags.shape[0]
    pair = pltpu.SemaphoreType.DMA((halves,))
    table = pltpu.SemaphoreType.DMA((halves, count))
    pieces = pltpu.SemaphoreType.DMA((halves, max(split), count))
    return pl.pallas_call(
        functools.partial(turn_kernel, count, near_count, split, flights, early),
        out_shape=(
            jax.ShapeDtypeStruct((2, count, halves, length // AVG // count, depth, LANES), jnp.bfloat16),
            jax.ShapeDtypeStruct((2 * beam_count, 4 * station_count), jnp.bfloat16),
        ),
        in_specs=[scalars, scalars, anywhere] + [whole] * 8,
        out_specs=(pl.BlockSpec(memory_space=pl.ANY), whole),
        scratch_shapes=[
            pltpu.SMEM((length,), jnp.int32),
            pltpu.VMEM((halves, LANES), jnp.float32),
            pltpu.VMEM((beam_count, 2 * station_count), jnp.float32),
            pltpu.VMEM((halves, count, 2, inputs, length), jnp.bfloat16),
            pltpu.VMEM((sections, 2, count, inputs, LANES), jnp.float32),
            pltpu.VMEM((sections, count * inputs, 2 * LANES), jnp.float32),
            pltpu.VMEM((length, 2 * count * inputs), jnp.float32),
            pltpu.VMEM((length, 2 * count * inputs), jnp.float32),
            pltpu.VMEM((length // 8 * depth, LANES), jnp.float32),
            pltpu.VMEM((halves, length // 8, depth, LANES), jnp.bfloat16),
            pltpu.SemaphoreType.REGULAR,
            pair, table, table, pair, pieces, pieces, pieces, pieces,
        ],
        compiler_params=pltpu.CompilerParams(
            collective_id=0, has_side_effects=True, vmem_limit_bytes=60 * 2**20
        ),
        name="turn",
    )(order, flags, voltages, *tables, coefficients, twist_cos, twist_sin, jnp.asarray(w_high), jnp.asarray(w_low))


def parts_of(block):
    rows = block.reshape(-1, 16, LANES).astype(jnp.float32)
    return [
        rows[:, begin : begin + 8].reshape(-1, LANES).astype(jnp.bfloat16) for begin in (0, 8)
    ]


def correlate_kernel(scale, frame_count, side_ref, all_ref, beam_ref, vis_ref, power_ref, held, made, in_sems, out_sems):
    over_lanes = (((1,), (1,)), ((), ()))
    count = power_ref.shape[0]
    slots, batch = made.shape[:2]
    steps = held.shape[3] // batch
    side = side_ref[0]

    def fetch(step):
        place = pl.ds(step * batch, batch)
        return pltpu.make_async_copy(all_ref.at[:, :, :, place], held.at[:, :, :, place], in_sems.at[step])

    def store(step, group):
        slot = step % slots
        return pltpu.make_async_copy(
            made.at[slot, group], vis_ref.at[step * batch + group], out_sems.at[slot, group]
        )

    for step in range(steps):
        fetch(step).start()

    @pl.loop(0, steps)
    def _(step):
        fetch(step).wait()

        @pl.when(step >= slots)
        def _():
            for group in range(batch):
                store(step - slots, group).wait()

        slot = step % slots
        stacked = []
        for group in range(batch):
            own_re, own_im = parts_of(held[side, :, :, step * batch + group])
            re, im = parts_of(held[:, :, :, step * batch + group])
            both = jnp.concatenate([re, im], axis=1)
            left_re = jnp.concatenate([own_re, own_im], axis=1)
            left_im = jnp.concatenate([own_im, -own_re], axis=1)
            for part, left in enumerate((left_re, left_im)):
                made[slot, group, part] = scale * lax.dot_general(
                    left, both, over_lanes, preferred_element_type=jnp.float32
                )
            store(step, group).start()
            stacked.append(jnp.concatenate([re, im], axis=0))
        beam = jnp.dot(
            beam_ref[...], jnp.concatenate(stacked, axis=1), preferred_element_type=jnp.float32
        )
        energy = beam * beam
        total = energy[:count]
        for piece in range(1, energy.shape[0] // count):
            total = total + energy[piece * count : (piece + 1) * count]
        lane = lax.broadcasted_iota(jnp.int32, (count, LANES), 1)
        tiles = LANES // AVG // batch
        lanes = pl.ds(pl.multiple_of(step // tiles * LANES, LANES), LANES)
        merged = jnp.where(step % tiles == 0, 0.0, power_ref[:, lanes])
        for group in range(batch):
            part = total[:, group * LANES : (group + 1) * LANES]
            shift = AVG
            while shift < LANES:
                part = part + pltpu.roll(part, shift, 1)
                shift *= 2
            merged = jnp.where(lane // AVG == step % tiles * batch + group, part / frame_count, merged)
        power_ref[:, lanes] = merged

    for step in range(steps - slots, steps):
        for group in range(batch):
            store(step, group).wait()


def correlate(gathered, side, beam_rows, frame_count):
    sides, sources, halves, groups, depth, _ = gathered.shape
    rows = sources * halves * 8
    batch = math.gcd(groups, 4)
    beam_local = beam_rows.shape[0] // 4
    whole = pl.BlockSpec(memory_space=pltpu.VMEM)
    anywhere = pl.BlockSpec(memory_space=pl.ANY)
    return pl.pallas_call(
        functools.partial(correlate_kernel, 1.0 / math.sqrt(AVG * frame_count), frame_count),
        in_specs=[pl.BlockSpec(memory_space=pltpu.SMEM), anywhere, whole],
        out_specs=(anywhere, whole),
        out_shape=(
            jax.ShapeDtypeStruct((groups, 2, rows, sides * rows), jnp.float32),
            jax.ShapeDtypeStruct((beam_local, groups * AVG), jnp.float32),
        ),
        scratch_shapes=[
            pltpu.VMEM(gathered.shape, gathered.dtype),
            pltpu.VMEM((3, batch, 2, rows, sides * rows), jnp.float32),
            pltpu.SemaphoreType.DMA((groups // batch,)),
            pltpu.SemaphoreType.DMA((3, batch)),
        ],
        compiler_params=pltpu.CompilerParams(vmem_limit_bytes=60 * 2**20),
        name="correlate",
    )(side.reshape(1), gathered, beam_rows)


def fast_shards(voltages, station_flags, channel_order, beam_stations, beam_weight_re, beam_weight_im):
    local_inputs, frames, length = voltages.shape[1:]
    devices = lax.axis_size("wide")
    blocks = voltages.reshape(2, devices, 2, local_inputs // devices // 2, length)
    tables = [table.T for table in (beam_stations, beam_weight_re, beam_weight_im)]
    gathered, beam_rows = turn(blocks, channel_order, station_flags, tables, prototype(TAPS, length))
    visibilities, power = correlate(gathered, lax.axis_index("narrow"), beam_rows, devices * frames)
    return visibilities, power.T


def solution(mesh):
    def body(*args):
        local_inputs, frames, length = args[0].shape[1:]
        devices = mesh.shape["wide"]
        share = local_inputs // devices
        sections = length // LANES
        fits = (
            frames == 1
            and local_inputs % devices == 0
            and share == 16
            and mesh.shape["narrow"] == 2
            and devices * AVG == LANES
            and length % (LANES * devices) == 0
            and args[3].shape[0] % 32 == 0
            and args[1].shape[0] == local_inputs
            and sections & (sections - 1) == 0
        )
        return (fast_shards if fits else shards)(*args)

    return jax.shard_map(
        body,
        mesh=mesh,
        in_specs=(P(None, "narrow", "wide", None), P(), P(), P(), P(), P()),
        out_specs=(P("wide", None, "narrow", None), P("wide", "narrow")),
        check_vma=False,
    )
```

```python
import functools
import math

import jax
import jax.numpy as jnp
import numpy as np
from jax import lax
from jax.experimental import pallas as pl
from jax.experimental.pallas import tpu as pltpu
from jax.sharding import PartitionSpec as P

TAPS = 8
AVG = 8
LANES = 128


def prototype(tap_count, length):
    places = np.arange(tap_count * length)
    offsets = places / length - tap_count / 2.0
    window = 0.5 - 0.5 * np.cos(2.0 * np.pi * (places + 0.5) / (tap_count * length))
    return (np.sinc(offsets) * window).astype(np.float32).reshape(tap_count, length)


def dense_weights(selection, weight_re, weight_im, station_count):
    beam_count, pick_count = selection.shape
    beam_rows = lax.broadcasted_iota(jnp.int32, (beam_count, pick_count), 0)
    flat_index = (beam_rows * station_count + selection).reshape(-1)
    summed_re = jax.ops.segment_sum(
        weight_re.reshape(-1), flat_index, num_segments=beam_count * station_count
    )
    summed_im = jax.ops.segment_sum(
        weight_im.reshape(-1), flat_index, num_segments=beam_count * station_count
    )
    return (
        summed_re.reshape(beam_count, station_count).astype(jnp.bfloat16),
        summed_im.reshape(beam_count, station_count).astype(jnp.bfloat16),
    )


def transform(filtered):
    input_count, frame_count, length = (filtered.shape[1], filtered.shape[2], filtered.shape[3])
    section_size = math.isqrt(length)
    counter = jnp.arange(section_size, dtype=jnp.int32)
    products = counter[:, None] * counter[None, :]
    section_angle = 2.0 * math.pi / section_size * (products % section_size).astype(jnp.float32)
    twist_angle = 2.0 * math.pi / length * products.astype(jnp.float32)
    cosine = jnp.cos(section_angle)
    sine_table = jnp.sin(section_angle)
    twist_cos = jnp.cos(twist_angle)
    twist_sin = jnp.sin(twist_angle)
    mixing = jnp.concatenate(
        [
            jnp.concatenate([cosine, -sine_table], axis=1),
            jnp.concatenate([sine_table, cosine], axis=1),
        ],
        axis=0,
    )
    twist_scale = jnp.concatenate([twist_cos, twist_cos], axis=1)
    twist_cross = jnp.concatenate([twist_sin, -twist_sin], axis=1)
    sample_grid = filtered.reshape(2, input_count, frame_count, section_size, section_size)
    stacked = jnp.moveaxis(sample_grid, 0, 3).reshape(
        input_count, frame_count, section_size, 2 * section_size
    )
    first_pass = jnp.einsum("cn,ifnk->ifck", cosine, stacked, precision=lax.Precision.HIGHEST)
    second_pass = jnp.einsum("cn,ifnk->ifck", sine_table, stacked, precision=lax.Precision.HIGHEST)
    sectioned = first_pass + jnp.concatenate(
        [second_pass[..., section_size:], -second_pass[..., :section_size]], axis=-1
    )
    swapped = jnp.concatenate(
        [sectioned[..., section_size:], sectioned[..., :section_size]], axis=-1
    )
    twisted = sectioned * twist_scale + swapped * twist_cross
    result = jnp.einsum("ifck,kj->ifcj", twisted, mixing, precision=lax.Precision.HIGHEST)
    return result * (1.0 / math.sqrt(length))


def row_stack(grouped):
    part_re, part_im = (grouped[0], grouped[1])
    return jnp.stack(
        [jnp.stack([part_re, part_im], axis=2), jnp.stack([part_im, -part_re], axis=2)], axis=0
    )


def apply_taps_long(extended, coefficients, frame_count):
    result = jnp.zeros(extended.shape[:2] + (frame_count, extended.shape[3]), jnp.float32)
    for tap_index in range(TAPS):
        begin = TAPS - 1 - tap_index
        result = result + coefficients[tap_index] * extended[
            :, :, begin : begin + frame_count
        ].astype(jnp.float32)
    return result


def shards(voltages, station_flags, channel_order, beam_stations, beam_weight_re, beam_weight_im):
    local_inputs = voltages.shape[1]
    frame_count = voltages.shape[2]
    length = voltages.shape[3]
    section_size = math.isqrt(length)
    coefficients = prototype(TAPS, length)
    across = lax.all_to_all(voltages, "wide", split_axis=3, concat_axis=2, tiled=True)
    column_count = across.shape[3]
    total_frames = across.shape[2]
    own_coeffs = lax.dynamic_slice_in_dim(
        coefficients, lax.axis_index("wide") * column_count, column_count, axis=1
    )
    padded = jnp.pad(across, ((0, 0), (0, 0), (TAPS - 1, 0), (0, 0)))
    local_filtered = apply_taps_long(padded, own_coeffs, total_frames)
    filtered = lax.all_to_all(local_filtered, "wide", split_axis=2, concat_axis=3, tiled=True)
    spectrum = transform(filtered)
    layout = spectrum.reshape(local_inputs, frame_count, section_size, 2, section_size)
    layout = jnp.transpose(layout, (3, 0, 2, 4, 1)).reshape(2, local_inputs, length, frame_count)
    local_stations = local_inputs // 2
    own_flags = lax.dynamic_slice_in_dim(
        station_flags, lax.axis_index("narrow") * local_stations, local_stations
    )
    input_gain = jnp.repeat(own_flags, 2).astype(jnp.float32)
    rounded = (layout * input_gain[None, :, None, None]).astype(jnp.bfloat16)
    position = channel_order % section_size * section_size + channel_order // section_size
    chosen = (position[:, None] == jnp.arange(length)[None, :]).astype(jnp.bfloat16)
    spectra = jnp.einsum('pk,rikf->ripf', chosen, rounded)
    turned = lax.all_to_all(spectra, "wide", split_axis=2, concat_axis=3, tiled=True)
    local_channels = turned.shape[2]
    all_frames = turned.shape[3]
    group_count = local_channels // AVG
    contraction = AVG * all_frames
    grouped = turned.reshape(2, local_inputs, group_count, contraction)
    vis_scale = 1.0 / math.sqrt(contraction)
    matrix_re, matrix_im = dense_weights(
        beam_stations, beam_weight_re, beam_weight_im, station_flags.shape[0]
    )
    beam_block = jnp.stack(
        [jnp.stack([matrix_re, -matrix_im], axis=1), jnp.stack([matrix_im, matrix_re], axis=1)],
        axis=0,
    )
    narrow_count = lax.axis_size("narrow")
    beam_local = beam_block.shape[1] // narrow_count
    own_beams = lax.dynamic_slice_in_dim(
        beam_block, lax.axis_index("narrow") * beam_local, beam_local, axis=1
    )
    left_rows = row_stack(grouped)
    shard_piece = lax.all_gather(grouped, "narrow", axis=1, tiled=True)
    columns = jnp.einsum(
        "rivqk,qjvk->vrij", left_rows, shard_piece, preferred_element_type=jnp.float32
    )
    piece_stations = shard_piece.shape[1] // 2
    voices = shard_piece.reshape(2, piece_stations, 2, group_count, contraction)
    beam_running = jnp.einsum(
        "obps,pslvk->oblvk", own_beams, voices, preferred_element_type=jnp.float32
    )
    visibilities = columns * vis_scale
    beam_energy = jnp.sum(beam_running * beam_running, axis=(0, 2)).reshape(
        beam_local, group_count, AVG, all_frames
    )
    beam_energy = jnp.sum(beam_energy, axis=3).reshape(beam_local, local_channels) / all_frames
    beam_power = beam_energy.T
    return (visibilities, beam_power)


def phase_table(rows, columns, period):
    products = np.arange(rows)[:, None] * np.arange(columns)[None, :]
    angle = 2.0 * np.pi / period * (products % period)
    return np.cos(angle).astype(np.float32), np.sin(angle).astype(np.float32)


def short_fft(parts):
    count = len(parts)
    if count == 1:
        return parts
    even = short_fft(parts[0::2])
    odd = short_fft(parts[1::2])
    low, high = [], []
    for place in range(count // 2):
        (even_re, even_im), (odd_re, odd_im) = even[place], odd[place]
        if place == 0:
            turn_re, turn_im = odd_re, odd_im
        elif 4 * place == count:
            turn_re, turn_im = odd_im, -odd_re
        else:
            cosine = math.cos(2.0 * math.pi * place / count)
            sine = math.sin(2.0 * math.pi * place / count)
            turn_re = cosine * odd_re + sine * odd_im
            turn_im = cosine * odd_im - sine * odd_re
        low.append((even_re + turn_re, even_im + turn_im))
        high.append((even_re - turn_re, even_im - turn_im))
    return low + high


def swap_octet(blocks):
    lane = lax.broadcasted_iota(jnp.int32, blocks[0].shape, 1)
    width = blocks[0].shape[1]
    for step in (1, 2, 4):
        keep = lane & step == 0
        swapped = list(blocks)
        for low in range(8):
            if low & step == 0:
                high = low + step
                swapped[low] = jnp.where(keep, blocks[low], pltpu.roll(blocks[high], step, 1))
                swapped[high] = jnp.where(keep, pltpu.roll(blocks[low], width - step, 1), blocks[high])
        blocks = swapped
    return blocks


def flip(place, mask, count):
    result, step = 0, 1
    while step < count:
        bit = place // step % 2
        result = result + step * (1 - bit if mask & step else bit)
        step *= 2
    return result


def channelize(half, hooks, refs, scratch):
    rows_ref, coef_ref, gain_ref, twist_cos_ref, twist_sin_ref, w_high_ref, w_low_ref = refs
    received, filt, stage, spec, picked, turned, spectra = scratch
    frames, _, inputs, length = received.shape[1:]
    sections = length // LANES
    hooks = list(hooks)

    def staged(total, pieces, unroll):
        size = total // pieces

        def run(body):
            for piece in range(pieces):
                pl.loop(piece * size, (piece + 1) * size, unroll=unroll)(body)
                if hooks:
                    hooks.pop(0)()

        return run

    @staged(sections, 2, 1)
    def _(section):
        lanes = pl.ds(pl.multiple_of(section * LANES, LANES), LANES)
        taps = [coef_ref[k : k + 1, lanes] for k in range(TAPS)]
        for part in range(2):
            window = []
            for frame in range(frames):
                window = [received[half, frame, part, :, lanes].astype(jnp.float32)] + window[: TAPS - 1]
                total = taps[0] * window[0]
                for k in range(1, len(window)):
                    total = total + taps[k] * window[k]
                filt[section, part, frame] = total

    @staged(frames, 2, 1)
    def _(frame):
        values = [(filt[s, 0, frame], filt[s, 1, frame]) for s in range(sections)]
        row = pl.multiple_of(frame * 8, 8)
        for c, (re, im) in enumerate(short_fft(values)):
            cosine, sine = twist_cos_ref[c : c + 1, :], twist_sin_ref[c : c + 1, :]
            stage[c, pl.ds(row, 8), :LANES] = re * cosine + im * sine
            stage[c, pl.ds(row, 8), LANES:] = im * cosine - re * sine

    over_lanes = (((1,), (1,)), ((), ()))

    @staged(sections, 2, 4)
    def _(c):
        value = stage[c]
        high = value.astype(jnp.bfloat16)
        low = (value - high.astype(jnp.float32)).astype(jnp.bfloat16)
        w_high, w_low = w_high_ref[...], w_low_ref[...]
        result = lax.dot_general(w_high, high, over_lanes, preferred_element_type=jnp.float32)
        result += lax.dot_general(w_high, low, over_lanes, preferred_element_type=jnp.float32)
        result += lax.dot_general(w_low, high, over_lanes, preferred_element_type=jnp.float32)
        result = result * gain_ref[half : half + 1, :]
        place = pl.ds(pl.multiple_of(c * LANES, LANES), LANES)
        spec[place, : frames * inputs] = result[:LANES]
        spec[place, frames * inputs :] = result[LANES:]

    @staged(length // 64, 2, 1)
    def _(step):
        base = pl.multiple_of(step * 64, 64)
        for begin in range(0, 64, 16):
            rows = [spec[pl.ds(rows_ref[base + begin + j], 1), :] for j in range(16)]
            for j, row in enumerate(rows):
                group, place = divmod(begin + j, 8)
                picked[pl.ds(base + place * 8 + group, 1), :] = row

    depth = 2 * inputs

    @staged(length // 64, 2, 2)
    def _(step):
        base = pl.multiple_of(step * 64, 64)
        target = pl.multiple_of(step * (8 * depth), 8 * depth)
        for part in range(2):
            lanes = slice(part * LANES, (part + 1) * LANES)
            blocks = [picked[pl.ds(base + place * 8, 8), lanes] for place in range(8)]
            for i, block in enumerate(swap_octet(blocks)):
                turned[pl.ds(target + part * inputs + i, 8, stride=depth), :] = block

    @staged(length // 64, 1, 4)
    def _(step):
        target = pl.multiple_of(step * (8 * depth), 8 * depth)
        rounded = turned[pl.ds(target, 8 * depth), :].astype(jnp.bfloat16)
        spectra[half, pl.ds(step * 8, 8)] = rounded.reshape(8, depth, LANES)

    for hook in hooks:
        hook()


def beam_rows_into(beam_ref, tables, side, sums):
    stations_ref, weight_re_ref, weight_im_ref = tables
    picks, beam_count = stations_ref.shape
    station_count = sums.shape[1] // 2
    place = lax.broadcasted_iota(jnp.int32, (station_count, beam_count), 0)

    def add(pick, totals):
        hit = place == stations_ref[pl.ds(pick, 1), :]
        return tuple(
            total + jnp.where(hit, ref[pl.ds(pick, 1), :], 0.0)
            for total, ref in zip(totals, (weight_re_ref, weight_im_ref))
        )

    zero = jnp.zeros((station_count, beam_count), jnp.float32)
    total_re, total_im = lax.fori_loop(0, picks, add, (zero, zero))
    sums[:, :station_count] = total_re.T
    sums[:, station_count:] = total_im.T
    own_count = beam_count // 2
    own = sums[pl.ds(pl.multiple_of(side * own_count, own_count), own_count), :].astype(jnp.bfloat16)
    matrix_re, matrix_im = own[:, :station_count], own[:, station_count:]
    inputs = 2 * station_count
    station = lax.broadcasted_iota(jnp.int32, (station_count, inputs), 0)
    column = lax.broadcasted_iota(jnp.int32, (station_count, inputs), 1)
    for polarization in range(2):
        spread = (column == 2 * station + polarization).astype(jnp.bfloat16)
        wide_re = jnp.dot(matrix_re, spread, preferred_element_type=jnp.float32)
        wide_im = jnp.dot(matrix_im, spread, preferred_element_type=jnp.float32)
        rows = pl.ds(polarization * own_count, own_count)
        beam_ref[rows, :inputs] = wide_re.astype(jnp.bfloat16)
        beam_ref[rows, inputs:] = (-wide_im).astype(jnp.bfloat16)
        rows = pl.ds((2 + polarization) * own_count, own_count)
        beam_ref[rows, :inputs] = wide_im.astype(jnp.bfloat16)
        beam_ref[rows, inputs:] = wide_re.astype(jnp.bfloat16)


def gain_into(gain, flags_ref, first):
    inputs = gain.shape[1] // 2
    pair = lax.broadcasted_iota(jnp.int32, (1, LANES), 1) % 8 // 2
    for half in range(2):
        row = jnp.zeros((1, LANES), jnp.int32)
        for k in range(4):
            row = jnp.where(pair == k, flags_ref[first + half * 4 + k], row)
        gain[half : half + 1, :] = row.astype(jnp.float32)


def rows_into(rows_ref, order_ref, sections):
    shift = sections.bit_length() - 1

    @pl.loop(0, order_ref.shape[0] // 16)
    def _(step):
        for j in range(16):
            channel = order_ref[step * 16 + j]
            rows_ref[step * 16 + j] = (channel & (sections - 1)) * LANES + (channel >> shift)


def turn_kernel(
    count, near_count, split, flights, early,
    order_ref, flags_ref, volt_ref, stations_ref, weight_re_ref, weight_im_ref,
    coef_ref, twist_cos_ref, twist_sin_ref, w_high_ref, w_low_ref,
    out_ref, beam_ref,
    rows_ref, gain_ref, sums, received, filt, stage, spec, picked, turned, spectra,
    hold, in_local, in_send, in_recv, out_local, out_send, out_recv, cross_send, cross_recv,
):
    me, side = lax.axis_index("wide"), lax.axis_index("narrow")
    mesh_ids = pl.DeviceIdType.MESH
    groups = spectra.shape[1] // count
    inputs = received.shape[3]
    barrier = pltpu.get_barrier_semaphore()
    for mask in range(1, count):
        pl.semaphore_signal(barrier, inc=1, device_id={"wide": flip(me, mask, count)}, device_id_type=mesh_ids)
    for mask in range(near_count):
        target = {"wide": flip(me, mask, count), "narrow": 1 - side}
        pl.semaphore_signal(barrier, inc=1, device_id=target, device_id_type=mesh_ids)
    pl.semaphore_wait(barrier, count - 1 + near_count)

    def entering(half, mask, back=False):
        peer = flip(me, mask, count)
        return pltpu.make_async_remote_copy(
            src_ref=volt_ref.at[:, peer, half],
            dst_ref=received.at[half, peer if back else me],
            send_sem=in_send.at[half, mask],
            recv_sem=in_recv.at[half, mask],
            device_id={"wide": peer},
            device_id_type=mesh_ids,
        )

    def kept_in(half):
        return pltpu.make_async_copy(volt_ref.at[:, me, half], received.at[half, me], in_local.at[half])

    def kept_out(half):
        return pltpu.make_async_copy(
            spectra.at[half, pl.ds(me * groups, groups)], out_ref.at[side, me, half], out_local.at[half]
        )

    def rows_of(half, mask, piece):
        size = groups // (split[half] if mask >= near_count else 1)
        return piece * size, size

    def outgoing(half, item, back=False):
        mask, piece = item
        begin, size = rows_of(half, mask, piece)
        peer = flip(me, mask, count)
        return pltpu.make_async_remote_copy(
            src_ref=spectra.at[half, pl.ds(peer * groups + begin, size)],
            dst_ref=out_ref.at[side, peer if back else me, half, pl.ds(begin, size)],
            send_sem=out_send.at[half, piece, mask],
            recv_sem=out_recv.at[half, piece, mask],
            device_id={"wide": peer},
            device_id_type=mesh_ids,
        )

    def across(half, item, back=False):
        mask, piece = item
        begin, size = rows_of(half, mask, piece)
        peer = flip(me, mask, count)
        place = pl.ds(begin, size)
        target_side = 1 - side if back else side
        if mask < near_count:
            source = spectra.at[half, pl.ds(peer * groups, groups)]
            target = out_ref.at[target_side, peer if back else me, half, place]
            device = {"wide": peer, "narrow": 1 - side}
        else:
            source = out_ref.at[side, peer, half, place]
            target = out_ref.at[target_side, peer, half, place]
            device = {"narrow": 1 - side}
        return pltpu.make_async_remote_copy(
            src_ref=source,
            dst_ref=target,
            send_sem=cross_send.at[half, piece, mask],
            recv_sem=cross_recv.at[half, piece, mask],
            device_id=device,
            device_id_type=mesh_ids,
        )

    near = [(mask, 0) for mask in range(1, near_count)]
    later = list(range(near_count, count // 2)) + list(range(count // 2, count))
    orders = [[(mask, piece) for mask in later for piece in range(split[half])] for half in range(2)]
    entry = list(range(count // 2, count)) + list(range(1, count // 2))
    refs = (rows_ref, coef_ref, gain_ref, twist_cos_ref, twist_sin_ref, w_high_ref, w_low_ref)
    scratch = (received, filt, stage, spec, picked, turned, spectra)

    def leave(half):
        for item in orders[half][: flights[half]]:
            outgoing(half, item).start()
        for item in near:
            outgoing(half, item).start()
        for item in [(0, 0)] + near:
            across(half, item).start()
        kept_out(half).start()

    def pass_on(half, place):
        def step():
            order = orders[half]
            if place + flights[half] < len(order):
                outgoing(half, order[place]).wait_send()
                outgoing(half, order[place + flights[half]]).start()
            outgoing(half, order[place], True).wait_recv()
            across(half, order[place]).start()

        return step

    for mask in entry:
        entering(0, mask).start()
    for half in range(2):
        kept_in(half).start()
    beam_rows_into(beam_ref, (stations_ref, weight_re_ref, weight_im_ref), side, sums)
    gain_into(gain_ref, flags_ref, (side * count + me) * inputs)
    rows_into(rows_ref, order_ref, twist_cos_ref.shape[0])
    for mask in entry:
        entering(0, mask).wait_send()
    for mask in entry[:early]:
        entering(1, mask).start()
    for mask in entry:
        entering(0, mask, True).wait_recv()
    neighbour = {"wide": flip(me, count // 4, count)}
    pl.semaphore_signal(hold, inc=1, device_id=neighbour, device_id_type=mesh_ids)
    pl.semaphore_wait(hold, 1)
    for mask in entry[early:]:
        entering(1, mask).start()
    kept_in(0).wait()
    channelize(0, [], refs, scratch)
    leave(0)
    kept_in(1).wait()
    for mask in entry:
        entering(1, mask).wait_send()
    for mask in entry:
        entering(1, mask, True).wait_recv()
    forwards = [pass_on(0, place) for place in range(len(orders[0]))]
    beside = [lambda: None] * 3 + forwards[:8]
    channelize(1, beside, refs, scratch)
    leave(1)
    for forward in forwards[8:]:
        forward()
    for place in range(len(orders[1])):
        pass_on(1, place)()
    for half in range(2):
        kept_out(half).wait()
        for item in near:
            outgoing(half, item).wait_send()
            outgoing(half, item, True).wait_recv()
        for item in orders[half][max(0, len(orders[half]) - flights[half]) :]:
            outgoing(half, item).wait_send()
        for item in [(0, 0)] + near + orders[half]:
            across(half, item).wait_send()
            across(half, item, True).wait_recv()


def turn(voltages, order, flags, tables, coefficients, near_count=4, split=(1, 1), flights=(8, 4), early=3):
    _, count, halves, inputs, length = voltages.shape
    sections = length // LANES
    twist_cos, twist_sin = phase_table(sections, LANES, length)
    cosine, sine = phase_table(LANES, LANES, LANES)
    weights = np.concatenate(
        [np.concatenate([cosine, sine], axis=1), np.concatenate([-sine, cosine], axis=1)], axis=0
    ) / np.float32(math.sqrt(length))
    w_high = weights.astype(jnp.bfloat16)
    w_low = (weights - w_high.astype(np.float32)).astype(jnp.bfloat16)
    scalars = pl.BlockSpec(memory_space=pltpu.SMEM)
    whole = pl.BlockSpec(memory_space=pltpu.VMEM)
    anywhere = pl.BlockSpec(memory_space=pltpu.HBM)
    depth = 2 * inputs
    beam_count, station_count = tables[0].shape[1], flags.shape[0]
    pair = pltpu.SemaphoreType.DMA((halves,))
    table = pltpu.SemaphoreType.DMA((halves, count))
    pieces = pltpu.SemaphoreType.DMA((halves, max(split), count))
    return pl.pallas_call(
        functools.partial(turn_kernel, count, near_count, split, flights, early),
        out_shape=(
            jax.ShapeDtypeStruct((2, count, halves, length // AVG // count, depth, LANES), jnp.bfloat16),
            jax.ShapeDtypeStruct((2 * beam_count, 4 * station_count), jnp.bfloat16),
        ),
        in_specs=[scalars, scalars, anywhere] + [whole] * 8,
        out_specs=(pl.BlockSpec(memory_space=pl.ANY), whole),
        scratch_shapes=[
            pltpu.SMEM((length,), jnp.int32),
            pltpu.VMEM((halves, LANES), jnp.float32),
            pltpu.VMEM((beam_count, 2 * station_count), jnp.float32),
            pltpu.VMEM((halves, count, 2, inputs, length), jnp.bfloat16),
            pltpu.VMEM((sections, 2, count, inputs, LANES), jnp.float32),
            pltpu.VMEM((sections, count * inputs, 2 * LANES), jnp.float32),
            pltpu.VMEM((length, 2 * count * inputs), jnp.float32),
            pltpu.VMEM((length, 2 * count * inputs), jnp.float32),
            pltpu.VMEM((length // 8 * depth, LANES), jnp.float32),
            pltpu.VMEM((halves, length // 8, depth, LANES), jnp.bfloat16),
            pltpu.SemaphoreType.REGULAR,
            pair, table, table, pair, pieces, pieces, pieces, pieces,
        ],
        compiler_params=pltpu.CompilerParams(
            collective_id=0, has_side_effects=True, vmem_limit_bytes=60 * 2**20
        ),
        name="turn",
    )(order, flags, voltages, *tables, coefficients, twist_cos, twist_sin, jnp.asarray(w_high), jnp.asarray(w_low))


def parts_of(block):
    rows = block.reshape(-1, 16, LANES).astype(jnp.float32)
    return [
        rows[:, begin : begin + 8].reshape(-1, LANES).astype(jnp.bfloat16) for begin in (0, 8)
    ]


def correlate_kernel(scale, frame_count, side_ref, all_ref, beam_ref, vis_ref, power_ref, held, made, in_sems, out_sems):
    over_lanes = (((1,), (1,)), ((), ()))
    count = power_ref.shape[0]
    slots, batch = made.shape[:2]
    steps = held.shape[3] // batch
    side = side_ref[0]

    def fetch(step):
        place = pl.ds(step * batch, batch)
        return pltpu.make_async_copy(all_ref.at[:, :, :, place], held.at[:, :, :, place], in_sems.at[step])

    def store(step, group):
        slot = step % slots
        return pltpu.make_async_copy(
            made.at[slot, group], vis_ref.at[step * batch + group], out_sems.at[slot, group]
        )

    for step in range(steps):
        fetch(step).start()

    @pl.loop(0, steps)
    def _(step):
        fetch(step).wait()

        @pl.when(step >= slots)
        def _():
            for group in range(batch):
                store(step - slots, group).wait()

        slot = step % slots
        stacked = []
        for group in range(batch):
            own_re, own_im = parts_of(held[side, :, :, step * batch + group])
            re, im = parts_of(held[:, :, :, step * batch + group])
            both = jnp.concatenate([re, im], axis=1)
            left_re = jnp.concatenate([own_re, own_im], axis=1)
            left_im = jnp.concatenate([own_im, -own_re], axis=1)
            for part, left in enumerate((left_re, left_im)):
                made[slot, group, part] = scale * lax.dot_general(
                    left, both, over_lanes, preferred_element_type=jnp.float32
                )
            store(step, group).start()
            stacked.append(jnp.concatenate([re, im], axis=0))
        beam = jnp.dot(
            beam_ref[...], jnp.concatenate(stacked, axis=1), preferred_element_type=jnp.float32
        )
        energy = beam * beam
        total = energy[:count]
        for piece in range(1, energy.shape[0] // count):
            total = total + energy[piece * count : (piece + 1) * count]
        lane = lax.broadcasted_iota(jnp.int32, (count, LANES), 1)
        tiles = LANES // AVG // batch
        lanes = pl.ds(pl.multiple_of(step // tiles * LANES, LANES), LANES)
        merged = jnp.where(step % tiles == 0, 0.0, power_ref[:, lanes])
        for group in range(batch):
            part = total[:, group * LANES : (group + 1) * LANES]
            shift = AVG
            while shift < LANES:
                part = part + pltpu.roll(part, shift, 1)
                shift *= 2
            merged = jnp.where(lane // AVG == step % tiles * batch + group, part / frame_count, merged)
        power_ref[:, lanes] = merged

    for step in range(steps - slots, steps):
        for group in range(batch):
            store(step, group).wait()


def correlate(gathered, side, beam_rows, frame_count):
    sides, sources, halves, groups, depth, _ = gathered.shape
    rows = sources * halves * 8
    batch = math.gcd(groups, 4)
    beam_local = beam_rows.shape[0] // 4
    whole = pl.BlockSpec(memory_space=pltpu.VMEM)
    anywhere = pl.BlockSpec(memory_space=pl.ANY)
    return pl.pallas_call(
        functools.partial(correlate_kernel, 1.0 / math.sqrt(AVG * frame_count), frame_count),
        in_specs=[pl.BlockSpec(memory_space=pltpu.SMEM), anywhere, whole],
        out_specs=(anywhere, whole),
        out_shape=(
            jax.ShapeDtypeStruct((groups, 2, rows, sides * rows), jnp.float32),
            jax.ShapeDtypeStruct((beam_local, groups * AVG), jnp.float32),
        ),
        scratch_shapes=[
            pltpu.VMEM(gathered.shape, gathered.dtype),
            pltpu.VMEM((3, batch, 2, rows, sides * rows), jnp.float32),
            pltpu.SemaphoreType.DMA((groups // batch,)),
            pltpu.SemaphoreType.DMA((3, batch)),
        ],
        compiler_params=pltpu.CompilerParams(vmem_limit_bytes=60 * 2**20),
        name="correlate",
    )(side.reshape(1), gathered, beam_rows)


def fast_shards(voltages, station_flags, channel_order, beam_stations, beam_weight_re, beam_weight_im):
    local_inputs, frames, length = voltages.shape[1:]
    devices = lax.axis_size("wide")
    blocks = voltages.reshape(2, devices, 2, local_inputs // devices // 2, length)
    tables = [table.T for table in (beam_stations, beam_weight_re, beam_weight_im)]
    gathered, beam_rows = turn(blocks, channel_order, station_flags, tables, prototype(TAPS, length))
    visibilities, power = correlate(gathered, lax.axis_index("narrow"), beam_rows, devices * frames)
    return visibilities, power.T


def solution(mesh):
    def body(*args):
        local_inputs, frames, length = args[0].shape[1:]
        devices = mesh.shape["wide"]
        share = local_inputs // devices
        sections = length // LANES
        fits = (
            frames == 1
            and local_inputs % devices == 0
            and share == 16
            and mesh.shape["narrow"] == 2
            and devices * AVG == LANES
            and length % (LANES * devices) == 0
            and args[3].shape[0] % 32 == 0
            and args[1].shape[0] == local_inputs
            and sections & (sections - 1) == 0
        )
        return (fast_shards if fits else shards)(*args)

    return jax.shard_map(
        body,
        mesh=mesh,
        in_specs=(P(None, "narrow", "wide", None), P(), P(), P(), P(), P()),
        out_specs=(P("wide", None, "narrow", None), P("wide", "narrow")),
        check_vma=False,
    )
```
